256 devices in a mesh: atoms: 32 (over x_hi, z, core), grid: 8 (over y, x_lo).
Axes of the slice: x: 4 (x_hi: 2, x_lo: 2; x = x_hi * 2 + x_lo), y: 4, z: 8, core: 2. Of those that a mesh axis runs over, the one named last changes fastest.
Arguments:
- basis_values: bfloat16 [32, 8, 2048, 1152], P('atoms', 'grid'), may hold values from -6 to 6
- potential: float32 [32, 8, 2048], P('atoms', 'grid'), may hold values from -6 to 6
- block_lists: int32 [32, 8, 6], P('atoms', 'grid'), may hold values from -1 to 8, as said below
Outputs:
- density_columns: float32 [32, 8, 768, 128], P('atoms', 'grid')
The draws below stay inside these ranges and needn't reach their ends.
Inputs may be any that keep to these rules, and one draw needn't show every extreme that they name: `block_lists`: entry 0 of every cell's list is 4, the cell itself. For some m from 4 to 6, entries 1 to m - 1 are distinct codes other than 4 whose neighbour cell lies on the line (line positions 0 to 7), and entries from m on are -1. Some cell has m = 6.
All inputs are finite; a program needn't handle non-finite values.
Results may differ from the reference program's by a relative error of at most 0.0017.
Values sent between devices are 32-bit elements; how exact they have to be, the bound alone decides.
A program may use at most 64 MiB of HBM per device.

```python
import jax
import jax.numpy as jnp
from jax import lax

B = 128
POINTS = 2048
MAXB = 6
ITERS = 3
REGIONS = 32
LINES = 8


def draw_block_lists(key, part):
    cell_total = REGIONS * LINES
    key_scores, key_counts = jax.random.split(jax.random.fold_in(key, 17))
    others = jnp.array([0, 1, 2, 3, 5, 6, 7, 8], dtype=jnp.int32)
    raw_scores = jax.random.randint(key_scores, (cell_total, 8), 0, 1 << 20, dtype=jnp.int32)
    scores = raw_scores * 16 + jnp.arange(8, dtype=jnp.int32)[None, :]
    line_pos = jnp.arange(cell_total, dtype=jnp.int32) % LINES
    reached = line_pos[:, None] + (others % 3 - 1)[None, :]
    outside = (reached < 0) | (reached >= LINES)
    scores = jnp.where(outside, scores - (1 << 26), scores)
    best_scores, best_index = lax.top_k(scores, 5)
    chosen = others[best_index]
    block_counts = jax.random.randint(key_counts, (cell_total,), MAXB - 2, MAXB + 1, dtype=jnp.int32)
    block_counts = block_counts.at[0].set(MAXB)
    slot_pos = jnp.arange(MAXB - 1, dtype=jnp.int32)
    tail_codes = jnp.where(slot_pos[None, :] < block_counts[:, None] - 1, chosen[:, :MAXB - 1], -1)
    code_lists = jnp.concatenate([jnp.full((cell_total, 1), 4, dtype=jnp.int32), tail_codes], axis=1)
    return code_lists.reshape(REGIONS, LINES, MAXB).astype(jnp.int32)


def steps_of(stream_key, dims, shards, smallest, top_value):
    level = 1.0
    for dim, parts in shards:
        heights = jax.random.uniform(jax.random.fold_in(jax.random.fold_in(stream_key, 6), dim), (parts,), jnp.float32, smallest / len(shards), top_value / len(shards))
        level = level * jnp.repeat(jnp.exp(heights), dims[dim] // parts).reshape((-1,) + (1,) * (len(dims) - 1 - dim))
    return level


def centred(rng, shape, width, reach, cuts=(), kind=jnp.bfloat16):
    loudness = steps_of(rng, shape, cuts, -0.22, 0.18) if cuts else 1.0
    entries = jax.random.normal(rng, shape, jnp.float32) * width * loudness
    return jnp.minimum(jnp.maximum(entries, -reach), reach).astype(kind)


def setup_inputs(seed: int = 0) -> dict:
    streams_of = jax.random.split(jax.random.key(seed), 4)
    basis_values = centred(streams_of[0], (REGIONS, LINES, POINTS, 9 * B), 1.0, 6.0, ((0, 32), (1, 8)))
    potential = centred(streams_of[1], (REGIONS, LINES, POINTS), 1.0, 6.0, ((0, 32), (1, 8)), jnp.float32)
    block_lists = draw_block_lists(jax.random.fold_in(streams_of[3], 71), 0)
    return {"basis_values": basis_values, "potential": potential, "block_lists": block_lists}


def newton_sign(submatrix, live_blocks, block_size):
    padded = submatrix.shape[0]
    position = jnp.arange(padded, dtype=jnp.int32)
    active = (position // block_size < live_blocks).astype(jnp.float32)
    live_count = (live_blocks * block_size).astype(jnp.float32)
    mean_level = jnp.trace(submatrix) / live_count
    shifted = (mean_level * jnp.diag(active) - submatrix) * active[:, None] * active[None, :]
    normal_form = shifted * (lax.rsqrt(jnp.sum(shifted * shifted) + 1e-06) * jnp.sqrt(live_count))
    square_form = jnp.dot(normal_form, normal_form, precision=lax.Precision.HIGHEST)
    fourth_form = jnp.dot(square_form, square_form, precision=lax.Precision.HIGHEST)
    bound_value = jnp.sqrt(jnp.sqrt(jnp.sqrt(jnp.sum(fourth_form * fourth_form) + 1e-06)))
    current = normal_form / bound_value
    square = square_form / (bound_value * bound_value)
    for sweep in range(ITERS - 1):
        if sweep > 0:
            square = jnp.dot(current, current, precision=lax.Precision.HIGHEST)
        current = 1.5 * current - 0.5 * jnp.dot(current, square, precision=lax.Precision.HIGHEST)
    columns = current[:, :block_size]
    inner_cols = jnp.dot(current, columns, precision=lax.Precision.HIGHEST)
    sign_cols = 1.5 * columns - 0.5 * jnp.dot(current, inner_cols, precision=lax.Precision.HIGHEST)
    unit_cols = (position[:, None] == jnp.arange(block_size, dtype=jnp.int32)[None, :]).astype(jnp.float32)
    return 0.5 * (unit_cols + sign_cols)

def cell_partial(operands):
    values, potential_cell = operands
    weighted = (values.astype(jnp.float32) * potential_cell[:, None]).astype(jnp.bfloat16)
    return lax.dot_general(weighted, values, (((0,), (0,)), ((), ())), preferred_element_type=jnp.float32)

def reference(basis_values, potential, block_lists):
    block_size = basis_values.shape[3] // 9
    cell_total = REGIONS * LINES
    partial_all = lax.map(cell_partial, (basis_values.reshape(cell_total, POINTS, 9 * block_size), potential.reshape(cell_total, POINTS)))
    partial_all = partial_all.reshape(REGIONS, LINES, 9, block_size, 9, block_size)
    codes_flat = block_lists.reshape(cell_total, MAXB)

    def one_cell(operands):
        index, slot_codes = operands
        region = index // LINES
        line_pos = index % LINES
        block_rows = []
        for first in range(MAXB):
            row_blocks = []
            for second in range(MAXB):
                code_first = slot_codes[first]
                code_second = slot_codes[second]
                first_a = code_first // 3 - 1
                first_r = code_first % 3 - 1
                second_a = code_second // 3 - 1
                second_r = code_second % 3 - 1
                total = jnp.zeros((block_size, block_size), jnp.float32)
                for shift_a in (-1, 0, 1):
                    for shift_r in (-1, 0, 1):
                        source_a = (region + first_a - shift_a) % REGIONS
                        source_r = line_pos + first_r - shift_r
                        rel_a = second_a - first_a + shift_a
                        rel_r = second_r - first_r + shift_r
                        usable = (code_first >= 0) & (code_second >= 0) & (source_r >= 0) & (source_r < LINES)
                        usable = usable & (jnp.abs(rel_a) <= 1) & (jnp.abs(rel_r) <= 1)
                        rel_code = jnp.clip((rel_a + 1) * 3 + rel_r + 1, 0, 8).astype(jnp.int32)
                        tile_block = partial_all[source_a, jnp.clip(source_r, 0, LINES - 1).astype(jnp.int32), (shift_a + 1) * 3 + shift_r + 1, :, rel_code, :]
                        total = total + jnp.where(usable, tile_block, jnp.float32(0.0))
                row_blocks.append(total)
            block_rows.append(jnp.concatenate(row_blocks, axis=1))
        submatrix = jnp.concatenate(block_rows, axis=0)
        live_blocks = jnp.sum((slot_codes >= 0).astype(jnp.int32))
        return newton_sign(submatrix, live_blocks, block_size)
    result = lax.map(one_cell, (jnp.arange(cell_total, dtype=jnp.int32), codes_flat))
    return result.reshape(REGIONS, LINES, MAXB * block_size, block_size)
```

```python
import jax
import jax.numpy as jnp
from jax import lax
from jax.experimental import pallas as pl
from jax.experimental.pallas import tpu as pltpu
from jax.sharding import PartitionSpec as P

MAXB = 6
B = 128
MESH = pl.DeviceIdType.MESH
F32 = jnp.float32
BF16 = jnp.bfloat16

LEFT_ROWS, OWN_ROWS, RIGHT_ROWS, LEFT_PAIR, OWN_PAIR, WIDE_PAIR = 0, 6, 12, 18, 27, 36


def sym_index(i, j):
    return i * 3 + j - i * (i + 1) // 2


class PairType:
    def __init__(self, number, symmetric, base):
        self.number, self.symmetric, self.base = number, symmetric, base
        self.keys = [(i, j) for i in range(3) for j in range(3) if i <= j or not symmetric]
        self.down = [(1, 1), (0, 1)] + ([] if symmetric else [(1, 0)])
        self.up = [(1, 2)] + ([] if symmetric else [(2, 1)])

    def at(self, i, j):
        return sym_index(i, j) if self.symmetric else i * 3 + j


TYPES = [
    PairType(0, True, OWN_ROWS),
    PairType(1, False, OWN_PAIR),
    PairType(2, False, WIDE_PAIR),
]


def exchange_kernel(
    n_atoms, n_grid, values, potential, out,
    weighted, send_ll, send_rr, send_lc, q0, q1, q2,
    got_ll, got_rr, got_lc, got_down, got_up, got_mid, got_far_down, got_far_up, mid, far,
    send_sem, recv_sem,
):
    a = lax.axis_index("atoms")
    r = lax.axis_index("grid")
    left, right = lax.rem(a + n_atoms - 1, n_atoms), lax.rem(a + 1, n_atoms)
    below, above = jnp.maximum(r - 1, 0), jnp.minimum(r + 1, n_grid - 1)
    below2, above2 = jnp.maximum(r - 2, 0), jnp.minimum(r + 2, n_grid - 1)
    has_below, has_above = r >= 1, r < n_grid - 1
    has_below2, has_above2 = r >= 2, r < n_grid - 2

    barrier = pltpu.get_barrier_semaphore()
    for peer in (left, right):
        pl.semaphore_signal(barrier, inc=1, device_id=(peer, r), device_id_type=MESH)
    for exists, peer in ((has_below, below), (has_above, above), (has_below2, below2), (has_above2, above2)):
        @pl.when(exists)
        def _():
            pl.semaphore_signal(barrier, inc=1, device_id=(a, peer), device_id_type=MESH)
    peers = 2
    for exists in (has_below, has_above, has_below2, has_above2):
        peers = peers + jnp.where(exists, 1, 0)
    pl.semaphore_wait(barrier, peers)

    counter = [0]
    sent = []

    def copy(src, dst, device, exists=None, recv=None):
        n = counter[0]
        counter[0] += 1
        c = pltpu.make_async_remote_copy(
            src_ref=src, dst_ref=dst, send_sem=send_sem.at[n],
            recv_sem=recv_sem.at[n if recv is None else recv],
            device_id=device, device_id_type=MESH,
        )
        if exists is None:
            c.start()
        else:
            pl.when(exists)(c.start)
        sent.append((c, exists))
        return c, n

    def wait_for(c, exists=None):
        if exists is None:
            c.wait_recv()
        else:
            pl.when(exists)(c.wait_recv)

    def weigh(group):
        for part in range(4):
            rows = slice(part * 512, part * 512 + 512)
            turned = values[rows, group * 384:group * 384 + 384].T
            weighted[:, rows] = (turned.astype(F32) * potential[:, rows]).astype(BF16)

    def product(group, other, dst, symmetric):
        for i in range(3):
            first = i if symmetric else 0
            row = jnp.dot(
                weighted[i * B:i * B + B, :],
                values[:, other * 384 + first * B:other * 384 + 384],
                preferred_element_type=F32,
            )
            for j in range(first, 3):
                n = sym_index(i, j) if symmetric else i * 3 + j
                dst[n] = row[:, (j - first) * B:(j - first) * B + B]

    q = [q0, q1, q2]
    state = [dict() for _ in TYPES]

    def line_first(t):
        s, num, mine = state[t.number], t.number, q[t.number]
        s["fd"] = copy(mine.at[t.at(0, 0)], got_far_down.at[num], (a, below2), has_below2)
        s["down"] = [copy(mine.at[t.at(*key)], got_down.at[num * 3 + n], (a, below), has_below) for n, key in enumerate(t.down)]
        s["up"] = [copy(mine.at[t.at(*key)], got_up.at[num * 2 + n], (a, above), has_above) for n, key in enumerate(t.up)]

    def line_second(t):
        s, num, mine = state[t.number], t.number, q[t.number]
        wait_for(s["fd"][0], has_above2)
        mid[num] = mine[t.at(2, 2)] + got_far_down[num]
        s["mid"] = copy(mid.at[num], got_mid.at[num], (a, above), has_above)
        copy(mine.at[t.at(0, 0)], got_mid.at[num], (a, below), r == 1, s["mid"][1])
        wait_for(s["down"][0][0], has_above)
        far[num] = mine[t.at(2, 2)] + got_down[num * 3]
        s["fu"] = copy(far.at[num], got_far_up.at[num], (a, above2), has_above2)
        copy(mine.at[t.at(1, 1)], got_far_up.at[num], (a, above), r == 0, s["fu"][1])

    def line_last(t, done):
        s, num, mine = state[t.number], t.number, q[t.number]

        def put(key, value):
            out[t.base + t.at(*key)] = value
            done(t.at(*key))

        put((0, 2), mine[t.at(0, 2)])
        if not t.symmetric:
            put((2, 0), mine[t.at(2, 0)])
        put((2, 2), far[num] + got_far_down[num])
        for n, (i, j) in list(enumerate(t.down))[1:]:
            wait_for(s["down"][n][0], has_above)
            put((i + 1, j + 1), mine[t.at(i + 1, j + 1)] + got_down[num * 3 + n])
        for n, (i, j) in enumerate(t.up):
            wait_for(s["up"][n][0], has_below)
            put((i - 1, j - 1), mine[t.at(i - 1, j - 1)] + got_up[num * 2 + n])
        wait_for(s["mid"][0])
        put((1, 1), mine[t.at(1, 1)] + got_mid[num])
        wait_for(s["fu"][0], has_below)
        put((0, 0), mine[t.at(0, 0)] + got_far_up[num])

    t0, t1, t2 = TYPES
    zero = jnp.zeros((B, B), F32)

    @pl.when(jnp.logical_not(has_above2))
    def _():
        for num in range(3):
            got_far_down[num] = zero

    weigh(0)
    product(0, 2, q2, False)
    line_first(t2)
    product(0, 1, send_lc, False)
    lc = [copy(send_lc.at[n], got_lc.at[n], (left, r)) for n in range(9)]
    product(0, 0, send_ll, True)
    ll = [copy(send_ll.at[n], got_ll.at[n], (left, r)) for n in range(6)]
    weigh(2)
    product(2, 2, send_rr, True)
    rr = [copy(send_rr.at[n], got_rr.at[n], (right, r)) for n in range(6)]
    weigh(1)
    product(1, 2, q1, False)
    product(1, 1, q0, True)
    line_second(t2)
    for n in range(9):
        wait_for(lc[n][0])
        q1[n] = q1[n] + got_lc[n]
    line_first(t1)
    for n in range(6):
        wait_for(ll[n][0])
        wait_for(rr[n][0])
        q0[n] = q0[n] + got_ll[n] + got_rr[n]
    line_first(t0)
    line_second(t1)
    line_second(t0)
    arrivals = []

    def pass_pair(n):
        arrivals.append(copy(out.at[OWN_PAIR + n], out.at[LEFT_PAIR + n], (right, r)))

    def pass_rows(n):
        arrivals.append(copy(out.at[OWN_ROWS + n], out.at[RIGHT_ROWS + n], (left, r)))
        arrivals.append(copy(out.at[OWN_ROWS + n], out.at[LEFT_ROWS + n], (right, r)))

    line_last(t2, lambda n: None)
    line_last(t1, pass_pair)
    line_last(t0, pass_rows)
    for c, _ in arrivals:
        c.wait_recv()
    for c, exists in sent:
        if exists is None:
            c.wait_send()
        else:
            pl.when(exists)(c.wait_send)


COPIES = 21 + 3 * 4 + (2 + 1) + 2 * (3 + 2) + 21 + 6


def exchange(values, potential, n_atoms, n_grid):
    def blocks(n):
        return pltpu.VMEM((n, B, B), F32)

    vmem = pl.BlockSpec(memory_space=pltpu.VMEM)
    return pl.pallas_call(
        lambda *refs: exchange_kernel(n_atoms, n_grid, *refs),
        out_shape=jax.ShapeDtypeStruct((45, B, B), F32),
        in_specs=[vmem, vmem],
        out_specs=vmem,
        scratch_shapes=[
            pltpu.VMEM((3 * B, values.shape[0]), BF16),
            blocks(6), blocks(6), blocks(9), blocks(6), blocks(9), blocks(9),
            blocks(6), blocks(6), blocks(9), blocks(9), blocks(6), blocks(3), blocks(3), blocks(3), blocks(3), blocks(3),
            pltpu.SemaphoreType.DMA((COPIES,)),
            pltpu.SemaphoreType.DMA((COPIES,)),
        ],
        compiler_params=pltpu.CompilerParams(
            collective_id=0, has_side_effects=True, vmem_limit_bytes=48 << 20
        ),
        name="exchange",
    )(values, potential)


def split(x):
    high = x.astype(BF16)
    return high, (x - high.astype(F32)).astype(BF16)


def sign_kernel(codes, blocks, out, raw, nh, nl, sh, sl, xh, xl, x):
    n = MAXB * B
    live = jnp.int32(0)
    for s in range(MAXB):
        live = live + jnp.where(codes[s] >= 0, 1, 0)

    def block_of(first, second):
        a1, i = first // 3, lax.rem(first, 3)
        a2, j = second // 3, lax.rem(second, 3)
        same = 6 * a1 + i * 3 + j - i * (i + 1) // 2
        apart = jnp.where(a2 - a1 == 2, WIDE_PAIR, LEFT_PAIR + 9 * a1) + i * 3 + j
        return jnp.where(a1 == a2, same, apart)

    eye = lax.broadcasted_iota(jnp.int32, (B, B), 0) == lax.broadcasted_iota(jnp.int32, (B, B), 1)
    zero = jnp.zeros((B, B), F32)
    trace = jnp.zeros((1, 1), F32)
    for s in range(MAXB):
        for t in range(s, MAXB):
            cs, ct = jnp.maximum(codes[s], 0), jnp.maximum(codes[t], 0)
            used = codes[t] >= 0
            blk = jnp.where(used, blocks[block_of(jnp.minimum(cs, ct), jnp.maximum(cs, ct))], zero)
            if s == t:
                raw[s * B:s * B + B, s * B:s * B + B] = blk
                trace = trace + jnp.sum(jnp.where(eye, blk, 0.0), keepdims=True)
            else:
                turned = blk.T
                ordered = cs < ct
                raw[s * B:s * B + B, t * B:t * B + B] = jnp.where(ordered, blk, turned)
                raw[t * B:t * B + B, s * B:s * B + B] = jnp.where(ordered, turned, blk)
    count = jnp.full((1, 1), live * B, jnp.int32).astype(F32)
    mean = trace / count
    total = jnp.zeros((1, 1), F32)
    for s in range(MAXB):
        rows = slice(s * B, s * B + B)
        diagonal = jnp.where(eye, jnp.where(s < live, mean, 0.0), 0.0)
        raw[rows, rows] = raw[rows, rows] - diagonal
        part = raw[rows, :]
        total = total + jnp.sum(part * part, keepdims=True)
    scale = -lax.rsqrt(total + 1e-06) * jnp.sqrt(count)
    for s in range(MAXB):
        rows = slice(s * B, s * B + B)
        part = raw[rows, :] * scale
        raw[rows, :] = part
        nh[rows, :], nl[rows, :] = split(part)

    tall = 256

    def dot(p, q):
        return jnp.dot(p, q, preferred_element_type=F32)

    def dot3(ph, plo, rows, qh, qlo):
        return dot(ph[rows, :], qh[...]) + (dot(ph[rows, :], qlo[...]) + dot(plo[rows, :], qh[...]))

    def rows_of(i):
        return pl.ds(pl.multiple_of(i * tall, tall), tall)

    @pl.loop(0, n // tall)
    def _(i):
        rows = rows_of(i)
        sh[rows, :], sl[rows, :] = split(dot3(nh, nl, rows, nh, nl))

    def fourth(i, acc):
        f = dot(sh[rows_of(i), :], sh[...])
        return acc + jnp.sum(f * f, keepdims=True)

    norm = lax.fori_loop(0, n // tall, fourth, jnp.zeros((1, 1), F32))
    rho = jnp.sqrt(jnp.sqrt(jnp.sqrt(norm + 1e-06)))
    inverse = 1.0 / rho
    linear, cubic = 1.5 * inverse, 0.5 * inverse * inverse * inverse

    @pl.loop(0, n // tall)
    def _(i):
        rows = rows_of(i)
        new = linear * raw[rows, :] - cubic * dot3(nh, nl, rows, sh, sl)
        x[rows, :] = new
        xh[rows, :], xl[rows, :] = split(new)

    @pl.loop(0, n // tall)
    def _(i):
        rows = rows_of(i)
        sh[rows, :], sl[rows, :] = split(dot3(xh, xl, rows, xh, xl))

    @pl.loop(0, n // tall)
    def _(i):
        rows = rows_of(i)
        new = 1.5 * x[rows, :] - 0.5 * dot3(xh, xl, rows, sh, sl)
        raw[rows, :] = new
        nh[rows, :], nl[rows, :] = split(new)

    @pl.loop(0, n // tall)
    def _(i):
        rows = rows_of(i)
        sh[rows, :B], sl[rows, :B] = split(dot3(nh, nl, rows, nh.at[:, :B], nl.at[:, :B]))

    for i in range(n // tall):
        rows = slice(i * tall, i * tall + tall)
        sign = 1.5 * raw[rows, :B] - 0.5 * dot3(nh, nl, rows, sh.at[:, :B], sl.at[:, :B])
        if i == 0:
            at = lax.broadcasted_iota(jnp.int32, (tall, B), 0) == lax.broadcasted_iota(jnp.int32, (tall, B), 1)
            sign = sign + jnp.where(at, 1.0, 0.0)
        out[rows, :] = 0.5 * sign


def sign_columns(codes, blocks):
    n = MAXB * B
    vmem = pl.BlockSpec(memory_space=pltpu.VMEM)
    half = pltpu.VMEM((n, n), BF16)
    full = pltpu.VMEM((n, n), F32)
    return pl.pallas_call(
        sign_kernel,
        out_shape=jax.ShapeDtypeStruct((n, B), F32),
        in_specs=[pl.BlockSpec(memory_space=pltpu.SMEM), vmem],
        out_specs=vmem,
        scratch_shapes=[full, half, half, half, half, half, half, full],
        compiler_params=pltpu.CompilerParams(vmem_limit_bytes=40 << 20),
        name="sign_columns",
    )(codes, blocks)


def solution(mesh):
    n_atoms, n_grid = mesh.shape["atoms"], mesh.shape["grid"]

    def shards(basis_values, potential, block_lists):
        blocks = exchange(basis_values[0, 0], potential[0], n_atoms, n_grid)
        return sign_columns(block_lists[0, 0], blocks)[None, None]

    placed = (P("atoms", "grid", None, None), P("atoms", "grid", None), P("atoms", "grid", None))
    return jax.shard_map(
        shards, mesh=mesh, in_specs=placed, out_specs=P("atoms", "grid", None, None), check_vma=False
    )
```

```python
import jax
import jax.numpy as jnp
from jax import lax
from jax.experimental import pallas as pl
from jax.experimental.pallas import tpu as pltpu
from jax.sharding import PartitionSpec as P

MAXB = 6
B = 128
MESH = pl.DeviceIdType.MESH
F32 = jnp.float32
BF16 = jnp.bfloat16

LEFT_ROWS, OWN_ROWS, RIGHT_ROWS, LEFT_PAIR, OWN_PAIR, WIDE_PAIR = 0, 6, 12, 18, 27, 36


def sym_index(i, j):
    return i * 3 + j - i * (i + 1) // 2


class PairType:
    def __init__(self, number, symmetric, base):
        self.number, self.symmetric, self.base = number, symmetric, base
        self.keys = [(i, j) for i in range(3) for j in range(3) if i <= j or not symmetric]
        self.down = [(1, 1), (0, 1)] + ([] if symmetric else [(1, 0)])
        self.up = [(1, 2)] + ([] if symmetric else [(2, 1)])

    def at(self, i, j):
        return sym_index(i, j) if self.symmetric else i * 3 + j


TYPES = [
    PairType(0, True, OWN_ROWS),
    PairType(1, False, OWN_PAIR),
    PairType(2, False, WIDE_PAIR),
]


def exchange_kernel(
    n_atoms, n_grid, values, potential, out,
    weighted, send_ll, send_rr, send_lc, q0, q1, q2,
    got_ll, got_rr, got_lc, got_down, got_up, got_mid, got_far_down, got_far_up, mid, far,
    send_sem, recv_sem,
):
    a = lax.axis_index("atoms")
    r = lax.axis_index("grid")
    left, right = lax.rem(a + n_atoms - 1, n_atoms), lax.rem(a + 1, n_atoms)
    below, above = jnp.maximum(r - 1, 0), jnp.minimum(r + 1, n_grid - 1)
    below2, above2 = jnp.maximum(r - 2, 0), jnp.minimum(r + 2, n_grid - 1)
    has_below, has_above = r >= 1, r < n_grid - 1
    has_below2, has_above2 = r >= 2, r < n_grid - 2

    barrier = pltpu.get_barrier_semaphore()
    for peer in (left, right):
        pl.semaphore_signal(barrier, inc=1, device_id=(peer, r), device_id_type=MESH)
    for exists, peer in ((has_below, below), (has_above, above), (has_below2, below2), (has_above2, above2)):
        @pl.when(exists)
        def _():
            pl.semaphore_signal(barrier, inc=1, device_id=(a, peer), device_id_type=MESH)
    peers = 2
    for exists in (has_below, has_above, has_below2, has_above2):
        peers = peers + jnp.where(exists, 1, 0)
    pl.semaphore_wait(barrier, peers)

    counter = [0]
    sent = []

    def copy(src, dst, device, exists=None, recv=None):
        n = counter[0]
        counter[0] += 1
        c = pltpu.make_async_remote_copy(
            src_ref=src, dst_ref=dst, send_sem=send_sem.at[n],
            recv_sem=recv_sem.at[n if recv is None else recv],
            device_id=device, device_id_type=MESH,
        )
        if exists is None:
            c.start()
        else:
            pl.when(exists)(c.start)
        sent.append((c, exists))
        return c, n

    def wait_for(c, exists=None):
        if exists is None:
            c.wait_recv()
        else:
            pl.when(exists)(c.wait_recv)

    def weigh(group):
        for part in range(4):
            rows = slice(part * 512, part * 512 + 512)
            turned = values[rows, group * 384:group * 384 + 384].T
            weighted[:, rows] = (turned.astype(F32) * potential[:, rows]).astype(BF16)

    def product(group, other, dst, symmetric):
        for i in range(3):
            first = i if symmetric else 0
            row = jnp.dot(
                weighted[i * B:i * B + B, :],
                values[:, other * 384 + first * B:other * 384 + 384],
                preferred_element_type=F32,
            )
            for j in range(first, 3):
                n = sym_index(i, j) if symmetric else i * 3 + j
                dst[n] = row[:, (j - first) * B:(j - first) * B + B]

    q = [q0, q1, q2]
    state = [dict() for _ in TYPES]

    def line_first(t):
        s, num, mine = state[t.number], t.number, q[t.number]
        s["fd"] = copy(mine.at[t.at(0, 0)], got_far_down.at[num], (a, below2), has_below2)
        s["down"] = [copy(mine.at[t.at(*key)], got_down.at[num * 3 + n], (a, below), has_below) for n, key in enumerate(t.down)]
        s["up"] = [copy(mine.at[t.at(*key)], got_up.at[num * 2 + n], (a, above), has_above) for n, key in enumerate(t.up)]

    def line_second(t):
        s, num, mine = state[t.number], t.number, q[t.number]
        wait_for(s["fd"][0], has_above2)
        mid[num] = mine[t.at(2, 2)] + got_far_down[num]
        s["mid"] = copy(mid.at[num], got_mid.at[num], (a, above), has_above)
        copy(mine.at[t.at(0, 0)], got_mid.at[num], (a, below), r == 1, s["mid"][1])
        wait_for(s["down"][0][0], has_above)
        far[num] = mine[t.at(2, 2)] + got_down[num * 3]
        s["fu"] = copy(far.at[num], got_far_up.at[num], (a, above2), has_above2)
        copy(mine.at[t.at(1, 1)], got_far_up.at[num], (a, above), r == 0, s["fu"][1])

    def line_last(t, done):
        s, num, mine = state[t.number], t.number, q[t.number]

        def put(key, value):
            out[t.base + t.at(*key)] = value
            done(t.at(*key))

        put((0, 2), mine[t.at(0, 2)])
        if not t.symmetric:
            put((2, 0), mine[t.at(2, 0)])
        put((2, 2), far[num] + got_far_down[num])
        for n, (i, j) in list(enumerate(t.down))[1:]:
            wait_for(s["down"][n][0], has_above)
            put((i + 1, j + 1), mine[t.at(i + 1, j + 1)] + got_down[num * 3 + n])
        for n, (i, j) in enumerate(t.up):
            wait_for(s["up"][n][0], has_below)
            put((i - 1, j - 1), mine[t.at(i - 1, j - 1)] + got_up[num * 2 + n])
        wait_for(s["mid"][0])
        put((1, 1), mine[t.at(1, 1)] + got_mid[num])
        wait_for(s["fu"][0], has_below)
        put((0, 0), mine[t.at(0, 0)] + got_far_up[num])

    t0, t1, t2 = TYPES
    zero = jnp.zeros((B, B), F32)

    @pl.when(jnp.logical_not(has_above2))
    def _():
        for num in range(3):
            got_far_down[num] = zero

    weigh(0)
    product(0, 2, q2, False)
    line_first(t2)
    product(0, 1, send_lc, False)
    lc = [copy(send_lc.at[n], got_lc.at[n], (left, r)) for n in range(9)]
    product(0, 0, send_ll, True)
    ll = [copy(send_ll.at[n], got_ll.at[n], (left, r)) for n in range(6)]
    weigh(2)
    product(2, 2, send_rr, True)
    rr = [copy(send_rr.at[n], got_rr.at[n], (right, r)) for n in range(6)]
    weigh(1)
    product(1, 2, q1, False)
    product(1, 1, q0, True)
    line_second(t2)
    for n in range(9):
        wait_for(lc[n][0])
        q1[n] = q1[n] + got_lc[n]
    line_first(t1)
    for n in range(6):
        wait_for(ll[n][0])
        wait_for(rr[n][0])
        q0[n] = q0[n] + got_ll[n] + got_rr[n]
    line_first(t0)
    line_second(t1)
    line_second(t0)
    arrivals = []

    def pass_pair(n):
        arrivals.append(copy(out.at[OWN_PAIR + n], out.at[LEFT_PAIR + n], (right, r)))

    def pass_rows(n):
        arrivals.append(copy(out.at[OWN_ROWS + n], out.at[RIGHT_ROWS + n], (left, r)))
        arrivals.append(copy(out.at[OWN_ROWS + n], out.at[LEFT_ROWS + n], (right, r)))

    line_last(t2, lambda n: None)
    line_last(t1, pass_pair)
    line_last(t0, pass_rows)
    for c, _ in arrivals:
        c.wait_recv()
    for c, exists in sent:
        if exists is None:
            c.wait_send()
        else:
            pl.when(exists)(c.wait_send)


COPIES = 21 + 3 * 4 + (2 + 1) + 2 * (3 + 2) + 21 + 6


def exchange(values, potential, n_atoms, n_grid):
    def blocks(n):
        return pltpu.VMEM((n, B, B), F32)

    vmem = pl.BlockSpec(memory_space=pltpu.VMEM)
    return pl.pallas_call(
        lambda *refs: exchange_kernel(n_atoms, n_grid, *refs),
        out_shape=jax.ShapeDtypeStruct((45, B, B), F32),
        in_specs=[vmem, vmem],
        out_specs=vmem,
        scratch_shapes=[
            pltpu.VMEM((3 * B, values.shape[0]), BF16),
            blocks(6), blocks(6), blocks(9), blocks(6), blocks(9), blocks(9),
            blocks(6), blocks(6), blocks(9), blocks(9), blocks(6), blocks(3), blocks(3), blocks(3), blocks(3), blocks(3),
            pltpu.SemaphoreType.DMA((COPIES,)),
            pltpu.SemaphoreType.DMA((COPIES,)),
        ],
        compiler_params=pltpu.CompilerParams(
            collective_id=0, has_side_effects=True, vmem_limit_bytes=48 << 20
        ),
        name="exchange",
    )(values, potential)


def sign_kernel(codes, blocks, out, raw, low, square, x):
    n = MAXB * B
    live = jnp.int32(0)
    for s in range(MAXB):
        live = live + jnp.where(codes[s] >= 0, 1, 0)

    def block_of(first, second):
        a1, i = first // 3, lax.rem(first, 3)
        a2, j = second // 3, lax.rem(second, 3)
        same = 6 * a1 + i * 3 + j - i * (i + 1) // 2
        apart = jnp.where(a2 - a1 == 2, WIDE_PAIR, LEFT_PAIR + 9 * a1) + i * 3 + j
        return jnp.where(a1 == a2, same, apart)

    eye = lax.broadcasted_iota(jnp.int32, (B, B), 0) == lax.broadcasted_iota(jnp.int32, (B, B), 1)
    zero = jnp.zeros((B, B), F32)
    diagonal = jnp.zeros((B, B), F32)
    for s in range(MAXB):
        cs = jnp.maximum(codes[s], 0)
        diagonal = diagonal + jnp.where(codes[s] >= 0, blocks[block_of(cs, cs)], zero)
    trace = jnp.sum(jnp.where(eye, diagonal, zero), keepdims=True)
    count = jnp.full((1, 1), live * B, jnp.int32).astype(F32)
    mean = trace / count
    once, twice = zero, zero
    for s in range(MAXB):
        for t in range(s, MAXB):
            cs, ct = jnp.maximum(codes[s], 0), jnp.maximum(codes[t], 0)
            used = codes[t] >= 0
            blk = jnp.where(used, blocks[block_of(jnp.minimum(cs, ct), jnp.maximum(cs, ct))], zero)
            rows, cols = slice(s * B, s * B + B), slice(t * B, t * B + B)
            if s == t:
                blk = blk - jnp.where(eye, jnp.where(used, mean, 0.0), zero)
                once = once + blk * blk
                raw[rows, cols] = blk
                low[rows, cols] = blk.astype(BF16)
            else:
                turned = blk.T
                twice = twice + blk * blk
                ordered = cs < ct
                here, there = jnp.where(ordered, blk, turned), jnp.where(ordered, turned, blk)
                raw[rows, cols] = here
                raw[cols, rows] = there
                low[rows, cols] = here.astype(BF16)
                low[cols, rows] = there.astype(BF16)
    total = jnp.sum(once + 2.0 * twice, keepdims=True)
    scale = -lax.rsqrt(total + 1e-06) * jnp.sqrt(count)
    tall = 256
    bands = [slice(i * tall, i * tall + tall) for i in range(n // tall)]

    def dot(p, q):
        return jnp.dot(p, q, preferred_element_type=F32)

    for rows in bands:
        square[rows, :] = (scale * scale * dot(low[rows, :], low[...])).astype(BF16)
    norm = jnp.zeros((1, 1), F32)
    for i, rows in enumerate(bands):
        f = dot(square[rows, :], square[:, i * tall:])
        norm = norm + jnp.sum(f[:, :tall] * f[:, :tall], keepdims=True)
        if i + 1 < len(bands):
            norm = norm + 2.0 * jnp.sum(f[:, tall:] * f[:, tall:], keepdims=True)
    rho = jnp.sqrt(jnp.sqrt(jnp.sqrt(norm + 1e-06)))
    inverse = 1.0 / rho
    linear, cubic = 1.5 * inverse * scale, 0.5 * inverse * inverse * inverse * scale
    for rows in bands:
        new = linear * raw[rows, :] - cubic * dot(low[rows, :], square[...])
        x[rows, :] = new
    for rows in bands:
        low[rows, :] = x[rows, :].astype(BF16)
    for rows in bands:
        square[rows, :] = dot(low[rows, :], low[...]).astype(BF16)
    for rows in bands:
        new = 1.5 * x[rows, :] - 0.5 * dot(low[rows, :], square[...])
        raw[rows, :B] = new[:, :B]
        x[rows, :] = new
    for rows in bands:
        low[rows, :] = x[rows, :].astype(BF16)
    for rows in bands:
        square[rows, :B] = dot(low[rows, :], low[:, :B]).astype(BF16)
    for i, rows in enumerate(bands):
        sign = 1.5 * raw[rows, :B] - 0.5 * dot(low[rows, :], square[:, :B])
        if i == 0:
            at = lax.broadcasted_iota(jnp.int32, (tall, B), 0) == lax.broadcasted_iota(jnp.int32, (tall, B), 1)
            sign = sign + jnp.where(at, 1.0, 0.0)
        out[rows, :] = 0.5 * sign


def sign_columns(codes, blocks):
    n = MAXB * B
    vmem = pl.BlockSpec(memory_space=pltpu.VMEM)
    half = pltpu.VMEM((n, n), BF16)
    full = pltpu.VMEM((n, n), F32)
    return pl.pallas_call(
        sign_kernel,
        out_shape=jax.ShapeDtypeStruct((n, B), F32),
        in_specs=[pl.BlockSpec(memory_space=pltpu.SMEM), vmem],
        out_specs=vmem,
        scratch_shapes=[full, half, half, full],
        compiler_params=pltpu.CompilerParams(vmem_limit_bytes=40 << 20),
        name="sign_columns",
    )(codes, blocks)


def solution(mesh):
    n_atoms, n_grid = mesh.shape["atoms"], mesh.shape["grid"]

    def shards(basis_values, potential, block_lists):
        blocks = exchange(basis_values[0, 0], potential[0], n_atoms, n_grid)
        return sign_columns(block_lists[0, 0], blocks)[None, None]

    placed = (P("atoms", "grid", None, None), P("atoms", "grid", None), P("atoms", "grid", None))
    return jax.shard_map(
        shards, mesh=mesh, in_specs=placed, out_specs=P("atoms", "grid", None, None), check_vma=False
    )
```

```python
import jax
import jax.numpy as jnp
from jax import lax
from jax.experimental import pallas as pl
from jax.experimental.pallas import tpu as pltpu
from jax.sharding import PartitionSpec as P

MAXB = 6
B = 128
MESH = pl.DeviceIdType.MESH
F32 = jnp.float32
BF16 = jnp.bfloat16

LEFT_ROWS, OWN_ROWS, RIGHT_ROWS, LEFT_PAIR, OWN_PAIR, WIDE_PAIR = 0, 6, 12, 18, 27, 36


def sym_index(i, j):
    return i * 3 + j - i * (i + 1) // 2


class PairType:
    def __init__(self, number, symmetric, base):
        self.number, self.symmetric, self.base = number, symmetric, base
        self.keys = [(i, j) for i in range(3) for j in range(3) if i <= j or not symmetric]
        self.down = [(1, 1), (0, 1)] + ([] if symmetric else [(1, 0)])
        self.up = [(1, 2)] + ([] if symmetric else [(2, 1)])

    def at(self, i, j):
        return sym_index(i, j) if self.symmetric else i * 3 + j


TYPES = [
    PairType(0, True, OWN_ROWS),
    PairType(1, False, OWN_PAIR),
    PairType(2, False, WIDE_PAIR),
]


def exchange_kernel(
    n_atoms, n_grid, values, potential, out,
    weighted, send_ll, send_rr, send_lc, q0, q1, q2,
    got_ll, got_rr, got_lc, got_down, got_up, got_mid, got_far_down, got_far_up, mid, far, v,
    send_sem, recv_sem, load_sem,
):
    loads = []
    for n, group in enumerate((0, 2, 1)):
        cols = slice(group * 384, group * 384 + 384)
        loads.append(pltpu.make_async_copy(values.at[:, cols], v.at[:, cols], load_sem.at[n]))
        loads[-1].start()
    a = lax.axis_index("atoms")
    r = lax.axis_index("grid")
    last = n_grid - 1
    half = n_atoms // 2
    left, right = lax.rem(a + n_atoms - 1, n_atoms), lax.rem(a + 1, n_atoms)
    below, above = jnp.maximum(r - 1, 0), jnp.minimum(r + 1, last)
    below2, above2 = jnp.maximum(r - 2, 0), jnp.minimum(r + 2, last)
    has_below, has_above = r >= 1, r < last
    has_below2, has_above2 = r >= 2, r < last - 1
    odd = lax.rem(r, 2) == 1
    even = jnp.logical_not(odd)
    first_half, last_half = lax.rem(a, half) == 0, lax.rem(a, half) == half - 1
    at_wrap = jnp.logical_or(first_half, last_half)
    across = jnp.where(first_half, left, right)

    barrier = pltpu.get_barrier_semaphore()
    for peer in (left, right):
        pl.semaphore_signal(barrier, inc=1, device_id=(peer, r), device_id_type=MESH)
    peers = 2
    for exists, peer in (
        (has_below, (a, below)), (has_above, (a, above)), (has_below2, (a, below2)), (has_above2, (a, above2)),
        (jnp.logical_and(at_wrap, has_below), (across, below)), (jnp.logical_and(at_wrap, has_above), (across, above)),
    ):
        @pl.when(exists)
        def _():
            pl.semaphore_signal(barrier, inc=1, device_id=peer, device_id_type=MESH)
        peers = peers + jnp.where(exists, 1, 0)
    pl.semaphore_wait(barrier, peers)

    next_send, next_recv = [0], [0]
    sent = []

    def receives(n):
        next_recv[0] += n
        return next_recv[0] - n

    def when(condition, step):
        if condition is None:
            step()
        else:
            pl.when(condition)(step)

    def copy(src, dst, device, exists, recv):
        c = pltpu.make_async_remote_copy(
            src_ref=src, dst_ref=dst, send_sem=send_sem.at[next_send[0]], recv_sem=recv_sem.at[recv],
            device_id=device, device_id_type=MESH,
        )
        next_send[0] += 1
        when(exists, c.start)
        sent.append((c, exists))

    def arrival(dst, recv):
        return pltpu.make_async_remote_copy(
            src_ref=mid.at[0], dst_ref=dst, send_sem=send_sem.at[0], recv_sem=recv_sem.at[recv],
            device_id=(right, r), device_id_type=MESH,
        )

    def valid(key):
        low, high = min(key) > 0, max(key) < 2
        if low and high:
            return None
        if low:
            return has_above
        return has_below if high else jnp.logical_and(has_below, has_above)

    def choose(wrapped, ours, theirs):
        ours = True if ours is None else ours
        theirs = True if theirs is None else theirs
        return jnp.logical_or(jnp.logical_and(wrapped, theirs), jnp.logical_and(jnp.logical_not(wrapped), ours))

    def other(key):
        if max(key) == 2 and min(key) == 0:
            return key, r
        if max(key) == 2:
            return (key[0] - 1, key[1] - 1), above
        return (key[0] + 1, key[1] + 1), below

    class Reduce:
        def __init__(self, src, got, t, peer, wrapped, receives_wrapped):
            self.src, self.got, self.t, self.peer = src, got, t, peer
            self.wrapped, self.receives_wrapped = wrapped, receives_wrapped
            self.extra = len(t.keys)
            self.recv = receives(self.extra + 1)

        def send(self, key):
            t = self.t
            slot = t.at(*key)
            if key == (1, 1):
                theirs = jnp.where(even, t.at(0, 0), t.at(2, 2))
                cell = jnp.where(even, above, below)
            else:
                moved, cell = other(key)
                theirs = self.extra if key == (0, 0) else t.at(*moved)
            to = jnp.where(self.wrapped, theirs, slot)
            copy(
                self.src.at[slot], self.got.at[to],
                (self.peer, jnp.where(self.wrapped, cell, r)), valid(key), self.recv + to,
            )

        def add(self, key, q):
            t = self.t
            slot = t.at(*key)
            ours = valid(key)
            theirs = {(0, 0): odd, (2, 2): even, (1, 1): has_below}.get(key, ours)
            arrives = ours if theirs is ours else choose(self.receives_wrapped, ours, theirs)

            def step():
                arrival(self.got.at[slot], self.recv + slot).wait_recv()
                q[slot] = q[slot] + self.got[slot]

            when(arrives, step)
            if key == (1, 1):
                @pl.when(jnp.logical_and(self.receives_wrapped, has_above))
                def _():
                    arrival(self.got.at[self.extra], self.recv + self.extra).wait_recv()
                    q[slot] = q[slot] + self.got[self.extra]

    class Gather:
        def __init__(self, t, base, peer, wrapped):
            self.t, self.base, self.peer, self.wrapped = t, base, peer, wrapped
            self.recv = receives(len(t.keys))

        def send(self, key):
            t = self.t
            src = out.at[t.base + t.at(*key)]

            def go(slot, cell, exists):
                copy(src, out.at[self.base + slot], (self.peer, cell), exists, self.recv + slot)

            slot = t.at(*key)
            if key == (1, 1):
                go(
                    jnp.where(self.wrapped, t.at(0, 0), slot), jnp.where(self.wrapped, above, r),
                    choose(self.wrapped, None, has_above),
                )
                go(t.at(2, 2), below, jnp.logical_and(self.wrapped, has_below))
                return
            moved, cell = other(key)
            ours = valid(key)
            theirs = {(0, 0): odd, (2, 2): even}.get(key, ours)
            go(
                jnp.where(self.wrapped, t.at(*moved), slot), jnp.where(self.wrapped, cell, r),
                ours if theirs is ours else choose(self.wrapped, ours, theirs),
            )

        def wait(self):
            for key in self.t.keys:
                slot = self.t.at(*key)
                when(valid(key), arrival(out.at[self.base + slot], self.recv + slot).wait_recv)

    def weigh(group):
        for part in range(4):
            rows = slice(part * 512, part * 512 + 512)
            turned = v[rows, group * 384:group * 384 + 384].T
            weighted[:, rows] = (turned.astype(F32) * potential[:, rows]).astype(BF16)

    def product(group, other, dst, symmetric):
        for i in range(3):
            first = i if symmetric else 0
            row = jnp.dot(
                weighted[i * B:i * B + B, :],
                v[:, other * 384 + first * B:other * 384 + 384],
                preferred_element_type=F32,
            )
            for j in range(first, 3):
                n = sym_index(i, j) if symmetric else i * 3 + j
                dst[n] = row[:, (j - first) * B:(j - first) * B + B]

    q = [q0, q1, q2]

    class Line:
        def __init__(self, t, done):
            self.t, self.done = t, done
            self.recv = receives(8)

        def first(self):
            t, num, mine, recv = self.t, self.t.number, q[self.t.number], self.recv
            copy(mine.at[t.at(0, 0)], got_far_down.at[num], (a, below2), has_below2, recv)
            for n, key in enumerate(t.down):
                copy(mine.at[t.at(*key)], got_down.at[num * 3 + n], (a, below), has_below, recv + 1 + n)
            for n, key in enumerate(t.up):
                copy(mine.at[t.at(*key)], got_up.at[num * 2 + n], (a, above), has_above, recv + 4 + n)
            self.put((0, 2), mine[t.at(0, 2)])
            if not t.symmetric:
                self.put((2, 0), mine[t.at(2, 0)])

        def second(self):
            t, num, mine, recv = self.t, self.t.number, q[self.t.number], self.recv
            when(has_above2, arrival(got_far_down.at[num], recv).wait_recv)
            mid[num] = mine[t.at(2, 2)] + got_far_down[num]
            copy(mid.at[num], got_mid.at[num], (a, above), has_above, recv + 6)
            copy(mine.at[t.at(0, 0)], got_mid.at[num], (a, below), r == 1, recv + 6)
            when(has_above, arrival(got_down.at[num * 3], recv + 1).wait_recv)
            far[num] = mine[t.at(2, 2)] + got_down[num * 3]
            copy(far.at[num], got_far_up.at[num], (a, above2), has_above2, recv + 7)
            copy(mine.at[t.at(1, 1)], got_far_up.at[num], (a, above), r == 0, recv + 7)

        def put(self, key, value):
            out[self.t.base + self.t.at(*key)] = value
            self.done(key)

        def last(self):
            t, num, mine, recv = self.t, self.t.number, q[self.t.number], self.recv
            self.put((2, 2), far[num] + got_far_down[num])
            for n, (i, j) in list(enumerate(t.down))[1:]:
                when(has_above, arrival(got_down.at[num * 3 + n], recv + 1 + n).wait_recv)
                self.put((i + 1, j + 1), mine[t.at(i + 1, j + 1)] + got_down[num * 3 + n])
            for n, (i, j) in enumerate(t.up):
                when(has_below, arrival(got_up.at[num * 2 + n], recv + 4 + n).wait_recv)
                self.put((i - 1, j - 1), mine[t.at(i - 1, j - 1)] + got_up[num * 2 + n])
            arrival(got_mid.at[num], recv + 6).wait_recv()
            self.put((1, 1), mine[t.at(1, 1)] + got_mid[num])
            when(has_below, arrival(got_far_up.at[num], recv + 7).wait_recv)
            self.put((0, 0), mine[t.at(0, 0)] + got_far_up[num])

    t0, t1, t2 = TYPES
    pair_right = Gather(t1, LEFT_PAIR, right, last_half)
    rows_right = Gather(t0, LEFT_ROWS, right, last_half)
    rows_left = Gather(t0, RIGHT_ROWS, left, first_half)

    def rows_done(key):
        rows_right.send(key)
        rows_left.send(key)

    line0, line1, line2 = Line(t0, rows_done), Line(t1, pair_right.send), Line(t2, lambda key: None)
    lc = Reduce(send_lc, got_lc, t1, left, first_half, last_half)
    ll = Reduce(send_ll, got_ll, t0, left, first_half, last_half)
    rr = Reduce(send_rr, got_rr, t0, right, last_half, first_half)

    @pl.when(jnp.logical_not(has_above2))
    def _():
        for num in range(3):
            got_far_down[num] = jnp.zeros((B, B), F32)

    loads[0].wait()
    weigh(0)
    loads[1].wait()
    product(0, 2, q2, False)
    line2.first()
    loads[2].wait()
    product(0, 1, send_lc, False)
    for key in t1.keys:
        lc.send(key)
    product(0, 0, send_ll, True)
    for key in t0.keys:
        ll.send(key)
    weigh(2)
    product(2, 2, send_rr, True)
    for key in t0.keys:
        rr.send(key)
    weigh(1)
    product(1, 2, q1, False)
    product(1, 1, q0, True)
    line2.second()
    for key in t1.keys:
        lc.add(key, q1)
    line1.first()
    for key in t0.keys:
        ll.add(key, q0)
        rr.add(key, q0)
    line0.first()
    line1.second()
    line0.second()
    line2.last()
    line1.last()
    line0.last()
    for gather in (pair_right, rows_right, rows_left):
        gather.wait()
    for c, exists in sent:
        when(exists, c.wait_send)


COPIES = 96


def exchange(values, potential, n_atoms, n_grid):
    def blocks(n):
        return pltpu.VMEM((n, B, B), F32)

    vmem = pl.BlockSpec(memory_space=pltpu.VMEM)
    return pl.pallas_call(
        lambda *refs: exchange_kernel(n_atoms, n_grid, *refs),
        out_shape=jax.ShapeDtypeStruct((45, B, B), F32),
        in_specs=[pl.BlockSpec(memory_space=pl.ANY), vmem],
        out_specs=vmem,
        scratch_shapes=[
            pltpu.VMEM((3 * B, values.shape[0]), BF16),
            blocks(6), blocks(6), blocks(9), blocks(6), blocks(9), blocks(9),
            blocks(7), blocks(7), blocks(10), blocks(9), blocks(6), blocks(3), blocks(3), blocks(3), blocks(3), blocks(3),
            pltpu.VMEM(values.shape, BF16),
            pltpu.SemaphoreType.DMA((COPIES,)),
            pltpu.SemaphoreType.DMA((COPIES,)),
            pltpu.SemaphoreType.DMA((3,)),
        ],
        compiler_params=pltpu.CompilerParams(
            collective_id=0, has_side_effects=True, vmem_limit_bytes=48 << 20
        ),
        name="exchange",
    )(values, potential)


def sign_kernel(codes, blocks, out, raw, low, square, x):
    n = MAXB * B
    live = jnp.int32(0)
    for s in range(MAXB):
        live = live + jnp.where(codes[s] >= 0, 1, 0)

    def block_of(first, second):
        a1, i = first // 3, lax.rem(first, 3)
        a2, j = second // 3, lax.rem(second, 3)
        same = 6 * a1 + i * 3 + j - i * (i + 1) // 2
        apart = jnp.where(a2 - a1 == 2, WIDE_PAIR, LEFT_PAIR + 9 * a1) + i * 3 + j
        return jnp.where(a1 == a2, same, apart)

    eye = lax.broadcasted_iota(jnp.int32, (B, B), 0) == lax.broadcasted_iota(jnp.int32, (B, B), 1)
    zero = jnp.zeros((B, B), F32)
    diagonal = jnp.zeros((B, B), F32)
    for s in range(MAXB):
        cs = jnp.maximum(codes[s], 0)
        diagonal = diagonal + jnp.where(codes[s] >= 0, blocks[block_of(cs, cs)], zero)
    trace = jnp.sum(jnp.where(eye, diagonal, zero), keepdims=True)
    count = jnp.full((1, 1), live * B, jnp.int32).astype(F32)
    mean = trace / count
    once, twice = zero, zero
    for s in range(MAXB):
        for t in range(s, MAXB):
            cs, ct = jnp.maximum(codes[s], 0), jnp.maximum(codes[t], 0)
            used = codes[t] >= 0
            blk = jnp.where(used, blocks[block_of(jnp.minimum(cs, ct), jnp.maximum(cs, ct))], zero)
            rows, cols = slice(s * B, s * B + B), slice(t * B, t * B + B)
            if s == t:
                blk = blk - jnp.where(eye, jnp.where(used, mean, 0.0), zero)
                once = once + blk * blk
                raw[rows, cols] = blk
                low[rows, cols] = blk.astype(BF16)
            else:
                turned = blk.T
                twice = twice + blk * blk
                ordered = cs < ct
                here, there = jnp.where(ordered, blk, turned), jnp.where(ordered, turned, blk)
                raw[rows, cols] = here
                raw[cols, rows] = there
                low[rows, cols] = here.astype(BF16)
                low[cols, rows] = there.astype(BF16)
    total = jnp.sum(once + 2.0 * twice, keepdims=True)
    scale = -lax.rsqrt(total + 1e-06) * jnp.sqrt(count)
    tall = 256
    bands = [slice(i * tall, i * tall + tall) for i in range(n // tall)]

    def dot(p, q):
        return jnp.dot(p, q, preferred_element_type=F32)

    for rows in bands:
        square[rows, :] = (scale * scale * dot(low[rows, :], low[...])).astype(BF16)
    norm = jnp.zeros((1, 1), F32)
    for i, rows in enumerate(bands):
        f = dot(square[rows, :], square[:, i * tall:])
        norm = norm + jnp.sum(f[:, :tall] * f[:, :tall], keepdims=True)
        if i + 1 < len(bands):
            norm = norm + 2.0 * jnp.sum(f[:, tall:] * f[:, tall:], keepdims=True)
    rho = jnp.sqrt(jnp.sqrt(jnp.sqrt(norm + 1e-06)))
    inverse = 1.0 / rho
    linear, cubic = 1.5 * inverse * scale, 0.5 * inverse * inverse * inverse * scale
    for rows in bands:
        new = linear * raw[rows, :] - cubic * dot(low[rows, :], square[...])
        x[rows, :] = new
    for rows in bands:
        low[rows, :] = x[rows, :].astype(BF16)
    for rows in bands:
        square[rows, :] = dot(low[rows, :], low[...]).astype(BF16)
    for rows in bands:
        new = 1.5 * x[rows, :] - 0.5 * dot(low[rows, :], square[...])
        raw[rows, :B] = new[:, :B]
        x[rows, :] = new
    for rows in bands:
        low[rows, :] = x[rows, :].astype(BF16)
    for rows in bands:
        square[rows, :B] = dot(low[rows, :], low[:, :B]).astype(BF16)
    for i, rows in enumerate(bands):
        sign = 1.5 * raw[rows, :B] - 0.5 * dot(low[rows, :], square[:, :B])
        if i == 0:
            at = lax.broadcasted_iota(jnp.int32, (tall, B), 0) == lax.broadcasted_iota(jnp.int32, (tall, B), 1)
            sign = sign + jnp.where(at, 1.0, 0.0)
        out[rows, :] = 0.5 * sign


def sign_columns(codes, blocks):
    n = MAXB * B
    vmem = pl.BlockSpec(memory_space=pltpu.VMEM)
    half = pltpu.VMEM((n, n), BF16)
    full = pltpu.VMEM((n, n), F32)
    return pl.pallas_call(
        sign_kernel,
        out_shape=jax.ShapeDtypeStruct((n, B), F32),
        in_specs=[pl.BlockSpec(memory_space=pltpu.SMEM), vmem],
        out_specs=vmem,
        scratch_shapes=[full, half, half, full],
        compiler_params=pltpu.CompilerParams(vmem_limit_bytes=40 << 20),
        name="sign_columns",
    )(codes, blocks)


def solution(mesh):
    n_atoms, n_grid = mesh.shape["atoms"], mesh.shape["grid"]

    def shards(basis_values, potential, block_lists):
        blocks = exchange(basis_values[0, 0], potential[0], n_atoms, n_grid)
        return sign_columns(block_lists[0, 0], blocks)[None, None]

    placed = (P("atoms", "grid", None, None), P("atoms", "grid", None), P("atoms", "grid", None))
    return jax.shard_map(
        shards, mesh=mesh, in_specs=placed, out_specs=P("atoms", "grid", None, None), check_vma=False
    )
```

```python
import jax
import jax.numpy as jnp
from jax import lax
from jax.experimental import pallas as pl
from jax.experimental.pallas import tpu as pltpu
from jax.sharding import PartitionSpec as P

MAXB = 6
B = 128
MESH = pl.DeviceIdType.MESH
F32 = jnp.float32
BF16 = jnp.bfloat16

LEFT_ROWS, OWN_ROWS, RIGHT_ROWS, LEFT_PAIR, OWN_PAIR, WIDE_PAIR = 0, 6, 12, 18, 27, 36


def sym_index(i, j):
    return i * 3 + j - i * (i + 1) // 2


class PairType:
    def __init__(self, number, symmetric, base):
        self.number, self.symmetric, self.base = number, symmetric, base
        self.keys = [(i, j) for i in range(3) for j in range(3) if i <= j or not symmetric]
        self.down = [(1, 1), (0, 1)] + ([] if symmetric else [(1, 0)])
        self.up = [(1, 2)] + ([] if symmetric else [(2, 1)])

    def at(self, i, j):
        return sym_index(i, j) if self.symmetric else i * 3 + j


TYPES = [
    PairType(0, True, OWN_ROWS),
    PairType(1, False, OWN_PAIR),
    PairType(2, False, WIDE_PAIR),
]


def exchange_kernel(
    n_atoms, n_grid, values, potential, out,
    weighted, send_ll, send_rr, send_lc, q0, q1, q2,
    got_ll, got_rr, got_lc, got_down, got_up, got_mid, got_far_down, got_far_up, mid, far, v,
    send_sem, recv_sem, load_sem,
):
    loads = []
    for n, group in enumerate((0, 2, 1)):
        cols = slice(group * 384, group * 384 + 384)
        loads.append(pltpu.make_async_copy(values.at[:, cols], v.at[:, cols], load_sem.at[n]))
        loads[-1].start()
    a = lax.axis_index("atoms")
    r = lax.axis_index("grid")
    last = n_grid - 1
    half = n_atoms // 2
    left, right = lax.rem(a + n_atoms - 1, n_atoms), lax.rem(a + 1, n_atoms)
    below, above = jnp.maximum(r - 1, 0), jnp.minimum(r + 1, last)
    below2, above2 = jnp.maximum(r - 2, 0), jnp.minimum(r + 2, last)
    has_below, has_above = r >= 1, r < last
    has_below2, has_above2 = r >= 2, r < last - 1
    odd = lax.rem(r, 2) == 1
    even = jnp.logical_not(odd)
    first_half, last_half = lax.rem(a, half) == 0, lax.rem(a, half) == half - 1
    at_wrap = jnp.logical_or(first_half, last_half)
    across = jnp.where(first_half, left, right)

    barrier = pltpu.get_barrier_semaphore()
    for peer in (left, right):
        pl.semaphore_signal(barrier, inc=1, device_id=(peer, r), device_id_type=MESH)
    peers = 2
    for exists, peer in (
        (has_below, (a, below)), (has_above, (a, above)), (has_below2, (a, below2)), (has_above2, (a, above2)),
        (jnp.logical_and(at_wrap, has_below), (across, below)), (jnp.logical_and(at_wrap, has_above), (across, above)),
    ):
        @pl.when(exists)
        def _():
            pl.semaphore_signal(barrier, inc=1, device_id=peer, device_id_type=MESH)
        peers = peers + jnp.where(exists, 1, 0)
    pl.semaphore_wait(barrier, peers)

    next_send, next_recv = [0], [0]
    sent = []

    def receives(n):
        next_recv[0] += n
        return next_recv[0] - n

    def when(condition, step):
        if condition is None:
            step()
        else:
            pl.when(condition)(step)

    def copy(src, dst, device, exists, recv):
        c = pltpu.make_async_remote_copy(
            src_ref=src, dst_ref=dst, send_sem=send_sem.at[next_send[0]], recv_sem=recv_sem.at[recv],
            device_id=device, device_id_type=MESH,
        )
        next_send[0] += 1
        when(exists, c.start)
        sent.append((c, exists))

    def arrival(dst, recv):
        return pltpu.make_async_remote_copy(
            src_ref=mid.at[0], dst_ref=dst, send_sem=send_sem.at[0], recv_sem=recv_sem.at[recv],
            device_id=(right, r), device_id_type=MESH,
        )

    def valid(key):
        low, high = min(key) > 0, max(key) < 2
        if low and high:
            return None
        if low:
            return has_above
        return has_below if high else jnp.logical_and(has_below, has_above)

    def choose(wrapped, ours, theirs):
        ours = True if ours is None else ours
        theirs = True if theirs is None else theirs
        return jnp.logical_or(jnp.logical_and(wrapped, theirs), jnp.logical_and(jnp.logical_not(wrapped), ours))

    def other(key):
        if max(key) == 2 and min(key) == 0:
            return key, r
        if max(key) == 2:
            return (key[0] - 1, key[1] - 1), above
        return (key[0] + 1, key[1] + 1), below

    class Reduce:
        def __init__(self, src, got, t, peer, wrapped, receives_wrapped):
            self.src, self.got, self.t, self.peer = src, got, t, peer
            self.wrapped, self.receives_wrapped = wrapped, receives_wrapped
            self.extra = len(t.keys)
            self.recv = receives(self.extra + 1)

        def send(self, key):
            t = self.t
            slot = t.at(*key)
            if key == (1, 1):
                theirs = jnp.where(even, t.at(0, 0), t.at(2, 2))
                cell = jnp.where(even, above, below)
            else:
                moved, cell = other(key)
                theirs = self.extra if key == (0, 0) else t.at(*moved)
            to = jnp.where(self.wrapped, theirs, slot)
            copy(
                self.src.at[slot], self.got.at[to],
                (self.peer, jnp.where(self.wrapped, cell, r)), valid(key), self.recv + to,
            )

        def add(self, key, q):
            t = self.t
            slot = t.at(*key)
            ours = valid(key)
            theirs = {(0, 0): odd, (2, 2): even, (1, 1): has_below}.get(key, ours)
            arrives = ours if theirs is ours else choose(self.receives_wrapped, ours, theirs)

            def step():
                arrival(self.got.at[slot], self.recv + slot).wait_recv()
                q[slot] = q[slot] + self.got[slot]

            when(arrives, step)
            if key == (1, 1):
                @pl.when(jnp.logical_and(self.receives_wrapped, has_above))
                def _():
                    arrival(self.got.at[self.extra], self.recv + self.extra).wait_recv()
                    q[slot] = q[slot] + self.got[self.extra]

    class Gather:
        def __init__(self, t, base, peer, wrapped):
            self.t, self.base, self.peer, self.wrapped = t, base, peer, wrapped
            self.recv = receives(len(t.keys))

        def send(self, key):
            t = self.t
            src = out.at[t.base + t.at(*key)]

            def go(slot, cell, exists):
                copy(src, out.at[self.base + slot], (self.peer, cell), exists, self.recv + slot)

            slot = t.at(*key)
            if key == (1, 1):
                go(
                    jnp.where(self.wrapped, t.at(0, 0), slot), jnp.where(self.wrapped, above, r),
                    choose(self.wrapped, None, has_above),
                )
                go(t.at(2, 2), below, jnp.logical_and(self.wrapped, has_below))
                return
            moved, cell = other(key)
            ours = valid(key)
            theirs = {(0, 0): odd, (2, 2): even}.get(key, ours)
            go(
                jnp.where(self.wrapped, t.at(*moved), slot), jnp.where(self.wrapped, cell, r),
                ours if theirs is ours else choose(self.wrapped, ours, theirs),
            )

        def wait(self):
            for key in self.t.keys:
                slot = self.t.at(*key)
                when(valid(key), arrival(out.at[self.base + slot], self.recv + slot).wait_recv)

    def weigh(group):
        for part in range(4):
            rows = slice(part * 512, part * 512 + 512)
            turned = v[rows, group * 384:group * 384 + 384].T
            weighted[:, rows] = (turned.astype(F32) * potential[:, rows]).astype(BF16)

    def product(group, other, dst, symmetric):
        block = jnp.dot(weighted[...], v[:, other * 384:other * 384 + 384], preferred_element_type=F32)
        for i in range(3):
            for j in range(i if symmetric else 0, 3):
                n = sym_index(i, j) if symmetric else i * 3 + j
                dst[n] = block[i * B:i * B + B, j * B:j * B + B]

    q = [q0, q1, q2]

    class Line:
        def __init__(self, t, done):
            self.t, self.done = t, done
            self.recv = receives(8)

        def start(self, key):
            t, num, mine, recv = self.t, self.t.number, q[self.t.number], self.recv
            src = mine.at[t.at(*key)]
            if key == (0, 0):
                copy(src, got_far_down.at[num], (a, below2), has_below2, recv)
                copy(src, got_mid.at[num], (a, below), r == 1, recv + 6)
            if key in t.down:
                n = t.down.index(key)
                copy(src, got_down.at[num * 3 + n], (a, below), has_below, recv + 1 + n)
            if key in t.up:
                n = t.up.index(key)
                copy(src, got_up.at[num * 2 + n], (a, above), has_above, recv + 4 + n)
            if key == (1, 1):
                copy(src, got_far_up.at[num], (a, above), r == 0, recv + 7)
            if key in ((0, 2), (2, 0)):
                self.put(key, src[...])

        def send_mid(self):
            t, num, mine, recv = self.t, self.t.number, q[self.t.number], self.recv
            when(has_above2, arrival(got_far_down.at[num], recv).wait_recv)
            mid[num] = mine[t.at(2, 2)] + got_far_down[num]
            copy(mid.at[num], got_mid.at[num], (a, above), has_above, recv + 6)

        def send_far(self):
            t, num, mine, recv = self.t, self.t.number, q[self.t.number], self.recv
            when(has_above, arrival(got_down.at[num * 3], recv + 1).wait_recv)
            far[num] = mine[t.at(2, 2)] + got_down[num * 3]
            copy(far.at[num], got_far_up.at[num], (a, above2), has_above2, recv + 7)

        def put(self, key, value):
            out[self.t.base + self.t.at(*key)] = value
            self.done(key)

        def sides(self):
            t, num, mine, recv = self.t, self.t.number, q[self.t.number], self.recv
            for n, (i, j) in list(enumerate(t.down))[1:]:
                when(has_above, arrival(got_down.at[num * 3 + n], recv + 1 + n).wait_recv)
                self.put((i + 1, j + 1), mine[t.at(i + 1, j + 1)] + got_down[num * 3 + n])
            for n, (i, j) in enumerate(t.up):
                when(has_below, arrival(got_up.at[num * 2 + n], recv + 4 + n).wait_recv)
                self.put((i - 1, j - 1), mine[t.at(i - 1, j - 1)] + got_up[num * 2 + n])

        def high(self):
            t, num = self.t, self.t.number
            self.put((2, 2), far[num] + got_far_down[num])

        def centre(self):
            t, num, mine, recv = self.t, self.t.number, q[self.t.number], self.recv
            arrival(got_mid.at[num], recv + 6).wait_recv()
            self.put((1, 1), mine[t.at(1, 1)] + got_mid[num])

        def low(self):
            t, num, mine, recv = self.t, self.t.number, q[self.t.number], self.recv
            when(has_below, arrival(got_far_up.at[num], recv + 7).wait_recv)
            self.put((0, 0), mine[t.at(0, 0)] + got_far_up[num])

    t0, t1, t2 = TYPES
    pair_right = Gather(t1, LEFT_PAIR, right, last_half)
    rows_right = Gather(t0, LEFT_ROWS, right, last_half)
    rows_left = Gather(t0, RIGHT_ROWS, left, first_half)

    def rows_done(key):
        rows_right.send(key)
        rows_left.send(key)

    line0, line1, line2 = Line(t0, rows_done), Line(t1, pair_right.send), Line(t2, lambda key: None)
    lc = Reduce(send_lc, got_lc, t1, left, first_half, last_half)
    ll = Reduce(send_ll, got_ll, t0, left, first_half, last_half)
    rr = Reduce(send_rr, got_rr, t0, right, last_half, first_half)

    @pl.when(jnp.logical_not(has_above2))
    def _():
        for num in range(3):
            got_far_down[num] = jnp.zeros((B, B), F32)

    def in_order(t):
        return [key for key in ((0, 0), (1, 1), (0, 1), (1, 0), (1, 2), (2, 1), (2, 2), (0, 2), (2, 0)) if key in t.keys]

    loads[0].wait()
    weigh(0)
    loads[1].wait()
    product(0, 2, q2, False)
    for key in in_order(t2):
        line2.start(key)
    product(0, 0, send_ll, True)
    for key in in_order(t0):
        ll.send(key)
    loads[2].wait()
    product(0, 1, send_lc, False)
    for key in in_order(t1):
        lc.send(key)
    weigh(2)
    product(2, 2, send_rr, True)
    for key in in_order(t0):
        rr.send(key)
    weigh(1)
    product(1, 1, q0, True)
    product(1, 2, q1, False)
    line2.send_far()
    for key in in_order(t0):
        ll.add(key, q0)
        rr.add(key, q0)
        line0.start(key)
    for key in in_order(t1):
        lc.add(key, q1)
        line1.start(key)
    line0.send_mid()
    line0.send_far()
    line1.send_mid()
    line2.send_mid()
    line0.sides()
    line0.high()
    line1.send_far()
    line1.sides()
    line1.high()
    line0.centre()
    line0.low()
    line1.centre()
    line1.low()
    line2.sides()
    line2.high()
    line2.centre()
    line2.low()
    for gather in (pair_right, rows_right, rows_left):
        gather.wait()
    for c, exists in sent:
        when(exists, c.wait_send)


COPIES = 96


def exchange(values, potential, n_atoms, n_grid):
    def blocks(n):
        return pltpu.VMEM((n, B, B), F32)

    vmem = pl.BlockSpec(memory_space=pltpu.VMEM)
    return pl.pallas_call(
        lambda *refs: exchange_kernel(n_atoms, n_grid, *refs),
        out_shape=jax.ShapeDtypeStruct((45, B, B), F32),
        in_specs=[pl.BlockSpec(memory_space=pl.ANY), vmem],
        out_specs=vmem,
        scratch_shapes=[
            pltpu.VMEM((3 * B, values.shape[0]), BF16),
            blocks(6), blocks(6), blocks(9), blocks(6), blocks(9), blocks(9),
            blocks(7), blocks(7), blocks(10), blocks(9), blocks(6), blocks(3), blocks(3), blocks(3), blocks(3), blocks(3),
            pltpu.VMEM(values.shape, BF16),
            pltpu.SemaphoreType.DMA((COPIES,)),
            pltpu.SemaphoreType.DMA((COPIES,)),
            pltpu.SemaphoreType.DMA((3,)),
        ],
        compiler_params=pltpu.CompilerParams(
            collective_id=0, has_side_effects=True, vmem_limit_bytes=48 << 20
        ),
        name="exchange",
    )(values, potential)


def sign_kernel(codes, blocks, out, raw, low, square, x):
    n = MAXB * B
    live = jnp.int32(0)
    for s in range(MAXB):
        live = live + jnp.where(codes[s] >= 0, 1, 0)

    def block_of(first, second):
        a1, i = first // 3, lax.rem(first, 3)
        a2, j = second // 3, lax.rem(second, 3)
        same = 6 * a1 + i * 3 + j - i * (i + 1) // 2
        apart = jnp.where(a2 - a1 == 2, WIDE_PAIR, LEFT_PAIR + 9 * a1) + i * 3 + j
        return jnp.where(a1 == a2, same, apart)

    eye = lax.broadcasted_iota(jnp.int32, (B, B), 0) == lax.broadcasted_iota(jnp.int32, (B, B), 1)
    zero = jnp.zeros((B, B), F32)
    diagonal = jnp.zeros((B, B), F32)
    for s in range(MAXB):
        cs = jnp.maximum(codes[s], 0)
        diagonal = diagonal + jnp.where(codes[s] >= 0, blocks[block_of(cs, cs)], zero)
    trace = jnp.sum(jnp.where(eye, diagonal, zero), keepdims=True)
    count = jnp.full((1, 1), live * B, jnp.int32).astype(F32)
    mean = trace / count
    once, twice = zero, zero
    for s in range(MAXB):
        for t in range(s, MAXB):
            cs, ct = jnp.maximum(codes[s], 0), jnp.maximum(codes[t], 0)
            used = codes[t] >= 0
            blk = jnp.where(used, blocks[block_of(jnp.minimum(cs, ct), jnp.maximum(cs, ct))], zero)
            rows, cols = slice(s * B, s * B + B), slice(t * B, t * B + B)
            if s == t:
                blk = blk - jnp.where(eye, jnp.where(used, mean, 0.0), zero)
                once = once + blk * blk
                raw[rows, cols] = blk
                low[rows, cols] = blk.astype(BF16)
            else:
                turned = blk.T
                twice = twice + blk * blk
                ordered = cs < ct
                here, there = jnp.where(ordered, blk, turned), jnp.where(ordered, turned, blk)
                raw[rows, cols] = here
                raw[cols, rows] = there
                low[rows, cols] = here.astype(BF16)
                low[cols, rows] = there.astype(BF16)
    total = jnp.sum(once + 2.0 * twice, keepdims=True)
    scale = -lax.rsqrt(total + 1e-06) * jnp.sqrt(count)
    tall = 256
    bands = [slice(i * tall, i * tall + tall) for i in range(n // tall)]

    def dot(p, q):
        return jnp.dot(p, q, preferred_element_type=F32)

    for rows in bands:
        square[rows, :] = (scale * scale * dot(low[rows, :], low[...])).astype(BF16)
    norm = jnp.zeros((1, 1), F32)
    for i, rows in enumerate(bands):
        f = dot(square[rows, :], square[:, i * tall:])
        norm = norm + jnp.sum(f[:, :tall] * f[:, :tall], keepdims=True)
        if i + 1 < len(bands):
            norm = norm + 2.0 * jnp.sum(f[:, tall:] * f[:, tall:], keepdims=True)
    rho = jnp.sqrt(jnp.sqrt(jnp.sqrt(norm + 1e-06)))
    inverse = 1.0 / rho
    linear, cubic = 1.5 * inverse * scale, 0.5 * inverse * inverse * inverse * scale
    for rows in bands:
        new = linear * raw[rows, :] - cubic * dot(low[rows, :], square[...])
        x[rows, :] = new
    for rows in bands:
        low[rows, :] = x[rows, :].astype(BF16)
    for rows in bands:
        square[rows, :] = dot(low[rows, :], low[...]).astype(BF16)
    for rows in bands:
        new = 1.5 * x[rows, :] - 0.5 * dot(low[rows, :], square[...])
        raw[rows, :B] = new[:, :B]
        x[rows, :] = new
    for rows in bands:
        low[rows, :] = x[rows, :].astype(BF16)
    for rows in bands:
        square[rows, :B] = dot(low[rows, :], low[:, :B]).astype(BF16)
    for i, rows in enumerate(bands):
        sign = 1.5 * raw[rows, :B] - 0.5 * dot(low[rows, :], square[:, :B])
        if i == 0:
            at = lax.broadcasted_iota(jnp.int32, (tall, B), 0) == lax.broadcasted_iota(jnp.int32, (tall, B), 1)
            sign = sign + jnp.where(at, 1.0, 0.0)
        out[rows, :] = 0.5 * sign


def sign_columns(codes, blocks):
    n = MAXB * B
    vmem = pl.BlockSpec(memory_space=pltpu.VMEM)
    half = pltpu.VMEM((n, n), BF16)
    full = pltpu.VMEM((n, n), F32)
    return pl.pallas_call(
        sign_kernel,
        out_shape=jax.ShapeDtypeStruct((n, B), F32),
        in_specs=[pl.BlockSpec(memory_space=pltpu.SMEM), vmem],
        out_specs=vmem,
        scratch_shapes=[full, half, half, full],
        compiler_params=pltpu.CompilerParams(vmem_limit_bytes=40 << 20),
        name="sign_columns",
    )(codes, blocks)


def solution(mesh):
    n_atoms, n_grid = mesh.shape["atoms"], mesh.shape["grid"]

    def shards(basis_values, potential, block_lists):
        blocks = exchange(basis_values[0, 0], potential[0], n_atoms, n_grid)
        return sign_columns(block_lists[0, 0], blocks)[None, None]

    placed = (P("atoms", "grid", None, None), P("atoms", "grid", None), P("atoms", "grid", None))
    return jax.shard_map(
        shards, mesh=mesh, in_specs=placed, out_specs=P("atoms", "grid", None, None), check_vma=False
    )
```

```python
import jax
import jax.numpy as jnp
from jax import lax
from jax.experimental import pallas as pl
from jax.experimental.pallas import tpu as pltpu
from jax.sharding import PartitionSpec as P

MAXB = 6
B = 128
MESH = pl.DeviceIdType.MESH
F32 = jnp.float32
BF16 = jnp.bfloat16

LEFT_ROWS, OWN_ROWS, RIGHT_ROWS, LEFT_PAIR, OWN_PAIR, WIDE_PAIR = 0, 6, 12, 18, 27, 36


def sym_index(i, j):
    return i * 3 + j - i * (i + 1) // 2


class PairType:
    def __init__(self, number, symmetric, base, distances):
        self.number, self.symmetric, self.base = number, symmetric, base
        self.size = 6 if symmetric else 9
        self.keys = [
            (i, j) for i in range(3) for j in range(3)
            if abs(i - j) in distances and (i <= j or not symmetric)
        ]
        self.down = [key for key in ((1, 1), (0, 1), (1, 0)) if key in self.keys]
        self.up = [key for key in ((1, 2), (2, 1)) if key in self.keys]

    def at(self, i, j):
        return sym_index(i, j) if self.symmetric else i * 3 + j


TYPES = [
    PairType(0, True, OWN_ROWS, (0, 1, 2)),
    PairType(1, False, OWN_PAIR, (0, 2)),
    PairType(2, False, WIDE_PAIR, (0, 1, 2)),
    PairType(3, False, LEFT_PAIR, (1,)),
]


def exchange_kernel(
    n_atoms, n_grid, values, potential, out,
    weighted, send_ll, send_rr, send_lc, send_cr, q0, q1, q2, q3,
    got_ll, got_rr, got_lc, got_cr, got_down, got_up, got_mid, got_far_down, got_far_up, mid, far, v,
    send_sem, recv_sem, load_sem,
):
    loads = []
    for n, group in enumerate((0, 2, 1)):
        cols = slice(group * 384, group * 384 + 384)
        loads.append(pltpu.make_async_copy(values.at[:, cols], v.at[:, cols], load_sem.at[n]))
        loads[-1].start()
    a = lax.axis_index("atoms")
    r = lax.axis_index("grid")
    last = n_grid - 1
    half = n_atoms // 2
    left, right = lax.rem(a + n_atoms - 1, n_atoms), lax.rem(a + 1, n_atoms)
    below, above = jnp.maximum(r - 1, 0), jnp.minimum(r + 1, last)
    below2, above2 = jnp.maximum(r - 2, 0), jnp.minimum(r + 2, last)
    has_below, has_above = r >= 1, r < last
    has_below2, has_above2 = r >= 2, r < last - 1
    odd = lax.rem(r, 2) == 1
    even = jnp.logical_not(odd)
    first_half, last_half = lax.rem(a, half) == 0, lax.rem(a, half) == half - 1
    at_wrap = jnp.logical_or(first_half, last_half)
    across = jnp.where(first_half, left, right)

    barrier = pltpu.get_barrier_semaphore()
    for peer in (left, right):
        pl.semaphore_signal(barrier, inc=1, device_id=(peer, r), device_id_type=MESH)
    peers = 2
    for exists, peer in (
        (has_below, (a, below)), (has_above, (a, above)), (has_below2, (a, below2)), (has_above2, (a, above2)),
        (jnp.logical_and(at_wrap, has_below), (across, below)), (jnp.logical_and(at_wrap, has_above), (across, above)),
    ):
        @pl.when(exists)
        def _():
            pl.semaphore_signal(barrier, inc=1, device_id=peer, device_id_type=MESH)
        peers = peers + jnp.where(exists, 1, 0)

    next_send, next_recv = [0], [0]
    sent = []

    def receives(n):
        next_recv[0] += n
        return next_recv[0] - n

    def when(condition, step):
        if condition is None:
            step()
        else:
            pl.when(condition)(step)

    def copy(src, dst, device, exists, recv):
        c = pltpu.make_async_remote_copy(
            src_ref=src, dst_ref=dst, send_sem=send_sem.at[next_send[0]], recv_sem=recv_sem.at[recv],
            device_id=device, device_id_type=MESH,
        )
        next_send[0] += 1
        when(exists, c.start)
        sent.append((c, exists))
        return sent[-1]

    def flush(copies):
        for entry in copies:
            c, exists = entry
            when(exists, c.wait_send)
            sent[:] = [other for other in sent if other is not entry]

    def arrival(dst, recv):
        return pltpu.make_async_remote_copy(
            src_ref=mid.at[0], dst_ref=dst, send_sem=send_sem.at[0], recv_sem=recv_sem.at[recv],
            device_id=(right, r), device_id_type=MESH,
        )

    def valid(key):
        low, high = min(key) > 0, max(key) < 2
        if low and high:
            return None
        if low:
            return has_above
        return has_below if high else jnp.logical_and(has_below, has_above)

    def choose(wrapped, ours, theirs):
        ours = True if ours is None else ours
        theirs = True if theirs is None else theirs
        return jnp.logical_or(jnp.logical_and(wrapped, theirs), jnp.logical_and(jnp.logical_not(wrapped), ours))

    def other(key):
        if max(key) == 2 and min(key) == 0:
            return key, r
        if max(key) == 2:
            return (key[0] - 1, key[1] - 1), above
        return (key[0] + 1, key[1] + 1), below

    class Reduce:
        def __init__(self, src, got, t, peer, wrapped, receives_wrapped):
            self.src, self.got, self.t, self.peer = src, got, t, peer
            self.wrapped, self.receives_wrapped = wrapped, receives_wrapped
            self.extra = t.size
            self.recv = receives(self.extra + 1)

        def send(self, key):
            t = self.t
            slot = t.at(*key)
            if key == (1, 1):
                theirs = jnp.where(even, t.at(0, 0), t.at(2, 2))
                cell = jnp.where(even, above, below)
            else:
                moved, cell = other(key)
                theirs = self.extra if key == (0, 0) else t.at(*moved)
            to = jnp.where(self.wrapped, theirs, slot)
            copy(
                self.src.at[slot], self.got.at[to],
                (self.peer, jnp.where(self.wrapped, cell, r)), valid(key), self.recv + to,
            )

        def add(self, key, q):
            t = self.t
            slot = t.at(*key)
            ours = valid(key)
            theirs = {(0, 0): odd, (2, 2): even, (1, 1): has_below}.get(key, ours)
            arrives = ours if theirs is ours else choose(self.receives_wrapped, ours, theirs)

            def step():
                arrival(self.got.at[slot], self.recv + slot).wait_recv()
                q[slot] = q[slot] + self.got[slot]

            when(arrives, step)
            if key == (1, 1):
                @pl.when(jnp.logical_and(self.receives_wrapped, has_above))
                def _():
                    arrival(self.got.at[self.extra], self.recv + self.extra).wait_recv()
                    q[slot] = q[slot] + self.got[self.extra]

    class Gather:
        def __init__(self, t, base, peer, wrapped):
            self.t, self.base, self.peer, self.wrapped = t, base, peer, wrapped
            self.recv = receives(t.size)

        def send(self, key):
            t = self.t
            src = out.at[t.base + t.at(*key)]

            def go(slot, cell, exists):
                copy(src, out.at[self.base + slot], (self.peer, cell), exists, self.recv + slot)

            slot = t.at(*key)
            if key == (1, 1):
                go(
                    jnp.where(self.wrapped, t.at(0, 0), slot), jnp.where(self.wrapped, above, r),
                    choose(self.wrapped, None, has_above),
                )
                go(t.at(2, 2), below, jnp.logical_and(self.wrapped, has_below))
                return
            moved, cell = other(key)
            ours = valid(key)
            theirs = {(0, 0): odd, (2, 2): even}.get(key, ours)
            go(
                jnp.where(self.wrapped, t.at(*moved), slot), jnp.where(self.wrapped, cell, r),
                ours if theirs is ours else choose(self.wrapped, ours, theirs),
            )

        def wait(self):
            for key in self.t.keys:
                slot = self.t.at(*key)
                when(valid(key), arrival(out.at[self.base + slot], self.recv + slot).wait_recv)

    def weigh(group):
        for part in range(4):
            rows = slice(part * 512, part * 512 + 512)
            turned = v[rows, group * 384:group * 384 + 384].T
            weighted[:, rows] = (turned.astype(F32) * potential[:, rows]).astype(BF16)

    def product(group, other, *places):
        block = jnp.dot(weighted[...], v[:, other * 384:other * 384 + 384], preferred_element_type=F32)
        for t, dst in places:
            for i, j in t.keys:
                dst[t.at(i, j)] = block[i * B:i * B + B, j * B:j * B + B]

    q = [q0, q1, q2, q3]

    class Line:
        def __init__(self, t, done):
            self.t, self.done = t, done
            self.recv = receives(8)

        def start(self, key):
            t, num, mine, recv = self.t, self.t.number, q[self.t.number], self.recv
            src = mine.at[t.at(*key)]
            started = []
            if key == (0, 0):
                copy(src, got_far_down.at[num], (a, below2), has_below2, recv)
                copy(src, got_mid.at[num], (a, below), r == 1, recv + 6)
            if key in t.down:
                n = t.down.index(key)
                started.append(copy(src, got_down.at[num * 3 + n], (a, below), has_below, recv + 1 + n))
            if key in t.up:
                n = t.up.index(key)
                started.append(copy(src, got_up.at[num * 2 + n], (a, above), has_above, recv + 4 + n))
            if key == (1, 1):
                copy(src, got_far_up.at[num], (a, above), r == 0, recv + 7)
            if key in ((0, 2), (2, 0)):
                self.put(key, src[...])
            return started

        def send_mid(self):
            t, num, mine, recv = self.t, self.t.number, q[self.t.number], self.recv
            when(has_above2, arrival(got_far_down.at[num], recv).wait_recv)
            mid[num] = mine[t.at(2, 2)] + got_far_down[num]
            return [copy(mid.at[num], got_mid.at[num], (a, above), has_above, recv + 6)]

        def send_far(self):
            t, num, mine, recv = self.t, self.t.number, q[self.t.number], self.recv
            when(has_above, arrival(got_down.at[num * 3], recv + 1).wait_recv)
            far[num] = mine[t.at(2, 2)] + got_down[num * 3]
            copy(far.at[num], got_far_up.at[num], (a, above2), has_above2, recv + 7)

        def put(self, key, value):
            out[self.t.base + self.t.at(*key)] = value
            self.done(key)

        def sides(self):
            t, num, mine, recv = self.t, self.t.number, q[self.t.number], self.recv
            for n, (i, j) in enumerate(t.down):
                if (i, j) == (1, 1):
                    continue
                when(has_above, arrival(got_down.at[num * 3 + n], recv + 1 + n).wait_recv)
                self.put((i + 1, j + 1), mine[t.at(i + 1, j + 1)] + got_down[num * 3 + n])
            for n, (i, j) in enumerate(t.up):
                when(has_below, arrival(got_up.at[num * 2 + n], recv + 4 + n).wait_recv)
                self.put((i - 1, j - 1), mine[t.at(i - 1, j - 1)] + got_up[num * 2 + n])

        def high(self):
            t, num = self.t, self.t.number
            self.put((2, 2), far[num] + got_far_down[num])

        def centre(self):
            t, num, mine, recv = self.t, self.t.number, q[self.t.number], self.recv
            arrival(got_mid.at[num], recv + 6).wait_recv()
            self.put((1, 1), mine[t.at(1, 1)] + got_mid[num])

        def low(self):
            t, num, mine, recv = self.t, self.t.number, q[self.t.number], self.recv
            when(has_below, arrival(got_far_up.at[num], recv + 7).wait_recv)
            self.put((0, 0), mine[t.at(0, 0)] + got_far_up[num])

    t0, t1, t2, t3 = TYPES
    pair_right = Gather(t1, LEFT_PAIR, right, last_half)
    pair_left = Gather(t3, OWN_PAIR, left, first_half)
    rows_right = Gather(t0, LEFT_ROWS, right, last_half)
    rows_left = Gather(t0, RIGHT_ROWS, left, first_half)

    def rows_done(key):
        rows_right.send(key)
        rows_left.send(key)

    line0, line1, line2 = Line(t0, rows_done), Line(t1, pair_right.send), Line(t2, lambda key: None)
    line3 = Line(t3, pair_left.send)
    lc = Reduce(send_lc, got_lc, t1, left, first_half, last_half)
    cr = Reduce(send_cr, got_cr, t3, right, last_half, first_half)
    ll = Reduce(send_ll, got_ll, t0, left, first_half, last_half)
    rr = Reduce(send_rr, got_rr, t0, right, last_half, first_half)

    @pl.when(jnp.logical_not(has_above2))
    def _():
        for num in range(3):
            got_far_down[num] = jnp.zeros((B, B), F32)

    def in_order(t):
        return [key for key in ((0, 0), (1, 1), (0, 1), (1, 0), (1, 2), (2, 1), (2, 2), (0, 2), (2, 0)) if key in t.keys]

    loads[0].wait()
    weigh(0)
    loads[1].wait()
    product(0, 2, (t2, q2))
    pl.semaphore_wait(barrier, peers)
    for key in in_order(t2):
        line2.start(key)
    product(0, 0, (t0, send_ll))
    for key in in_order(t0):
        ll.send(key)
    loads[2].wait()
    product(0, 1, (t1, send_lc), (t3, q3))
    for key in in_order(t1):
        lc.send(key)
    weigh(2)
    product(2, 2, (t0, send_rr))
    for key in in_order(t0):
        rr.send(key)
    weigh(1)
    product(1, 2, (t1, q1), (t3, send_cr))
    for key in in_order(t3):
        cr.send(key)
    product(1, 1, (t0, q0))
    line2.send_far()
    first = []
    for key in ((0, 0), (1, 1)):
        ll.add(key, q0)
        rr.add(key, q0)
        first += line0.start(key)
    for key in ((0, 0), (1, 1)):
        lc.add(key, q1)
        first += line1.start(key)
    for key in ((2, 2), (0, 1), (1, 2), (0, 2)):
        ll.add(key, q0)
        rr.add(key, q0)
    middle = line0.send_mid()
    for key in ((2, 2), (0, 2), (2, 0)):
        lc.add(key, q1)
    middle += line1.send_mid()
    line0.start((0, 2))
    line1.start((0, 2))
    line1.start((2, 0))
    for key in in_order(t3):
        cr.add(key, q3)
    flush(first)
    sides = []
    for key in ((0, 1), (1, 2)):
        sides += line0.start(key)
    for key in ((0, 1), (1, 0)):
        sides += line3.start(key)
    line0.send_far()
    line1.send_far()
    line0.high()
    line1.high()
    flush(middle)
    for key in ((1, 2), (2, 1)):
        line3.start(key)
    line0.centre()
    line1.centre()
    line0.low()
    line1.low()
    flush(sides)
    line2.send_mid()
    line0.sides()
    line3.sides()
    line2.sides()
    line2.high()
    line2.centre()
    line2.low()
    for gather in (pair_right, pair_left, rows_right, rows_left):
        gather.wait()
    for c, exists in sent:
        when(exists, c.wait_send)


COPIES = 128


def exchange(values, potential, n_atoms, n_grid):
    def blocks(n):
        return pltpu.VMEM((n, B, B), F32)

    vmem = pl.BlockSpec(memory_space=pltpu.VMEM)
    return pl.pallas_call(
        lambda *refs: exchange_kernel(n_atoms, n_grid, *refs),
        out_shape=jax.ShapeDtypeStruct((45, B, B), F32),
        in_specs=[pl.BlockSpec(memory_space=pl.ANY), vmem],
        out_specs=vmem,
        scratch_shapes=[
            pltpu.VMEM((3 * B, values.shape[0]), BF16),
            blocks(6), blocks(6), blocks(9), blocks(9), blocks(6), blocks(9), blocks(9), blocks(9),
            blocks(7), blocks(7), blocks(10), blocks(10), blocks(12), blocks(8), blocks(3), blocks(3), blocks(3), blocks(3), blocks(3),
            pltpu.VMEM(values.shape, BF16),
            pltpu.SemaphoreType.DMA((COPIES,)),
            pltpu.SemaphoreType.DMA((COPIES,)),
            pltpu.SemaphoreType.DMA((3,)),
        ],
        compiler_params=pltpu.CompilerParams(
            collective_id=0, has_side_effects=True, vmem_limit_bytes=48 << 20
        ),
        name="exchange",
    )(values, potential)


def sign_kernel(codes, blocks, out, raw, low, square, x):
    n = MAXB * B
    live = jnp.int32(0)
    for s in range(MAXB):
        live = live + jnp.where(codes[s] >= 0, 1, 0)

    def block_of(first, second):
        a1, i = first // 3, lax.rem(first, 3)
        a2, j = second // 3, lax.rem(second, 3)
        same = 6 * a1 + i * 3 + j - i * (i + 1) // 2
        apart = jnp.where(a2 - a1 == 2, WIDE_PAIR, LEFT_PAIR + 9 * a1) + i * 3 + j
        return jnp.where(a1 == a2, same, apart)

    eye = lax.broadcasted_iota(jnp.int32, (B, B), 0) == lax.broadcasted_iota(jnp.int32, (B, B), 1)
    zero = jnp.zeros((B, B), F32)
    diagonal = jnp.zeros((B, B), F32)
    for s in range(MAXB):
        cs = jnp.maximum(codes[s], 0)
        diagonal = diagonal + jnp.where(codes[s] >= 0, blocks[block_of(cs, cs)], zero)
    trace = jnp.sum(jnp.where(eye, diagonal, zero), keepdims=True)
    count = jnp.full((1, 1), live * B, jnp.int32).astype(F32)
    mean = trace / count
    once, twice = zero, zero
    for s in range(MAXB):
        for t in range(s, MAXB):
            cs, ct = jnp.maximum(codes[s], 0), jnp.maximum(codes[t], 0)
            used = codes[t] >= 0
            blk = jnp.where(used, blocks[block_of(jnp.minimum(cs, ct), jnp.maximum(cs, ct))], zero)
            rows, cols = slice(s * B, s * B + B), slice(t * B, t * B + B)
            if s == t:
                blk = blk - jnp.where(eye, jnp.where(used, mean, 0.0), zero)
                once = once + blk * blk
                raw[rows, cols] = blk
                low[rows, cols] = blk.astype(BF16)
            else:
                turned = blk.T
                twice = twice + blk * blk
                ordered = cs < ct
                here, there = jnp.where(ordered, blk, turned), jnp.where(ordered, turned, blk)
                raw[rows, cols] = here
                raw[cols, rows] = there
                low[rows, cols] = here.astype(BF16)
                low[cols, rows] = there.astype(BF16)
    total = jnp.sum(once + 2.0 * twice, keepdims=True)
    scale = -lax.rsqrt(total + 1e-06) * jnp.sqrt(count)
    tall = 256
    bands = [slice(i * tall, i * tall + tall) for i in range(n // tall)]

    def dot(p, q):
        return jnp.dot(p, q, preferred_element_type=F32)

    for rows in bands:
        square[rows, :] = (scale * scale * dot(low[rows, :], low[...])).astype(BF16)
    norm = jnp.zeros((1, 1), F32)
    for i, rows in enumerate(bands):
        f = dot(square[rows, :], square[:, i * tall:])
        norm = norm + jnp.sum(f[:, :tall] * f[:, :tall], keepdims=True)
        if i + 1 < len(bands):
            norm = norm + 2.0 * jnp.sum(f[:, tall:] * f[:, tall:], keepdims=True)
    rho = jnp.sqrt(jnp.sqrt(jnp.sqrt(norm + 1e-06)))
    inverse = 1.0 / rho
    linear, cubic = 1.5 * inverse * scale, 0.5 * inverse * inverse * inverse * scale
    for rows in bands:
        new = linear * raw[rows, :] - cubic * dot(low[rows, :], square[...])
        x[rows, :] = new
    for rows in bands:
        low[rows, :] = x[rows, :].astype(BF16)
    for rows in bands:
        square[rows, :] = dot(low[rows, :], low[...]).astype(BF16)
    for rows in bands:
        new = 1.5 * x[rows, :] - 0.5 * dot(low[rows, :], square[...])
        raw[rows, :B] = new[:, :B]
        x[rows, :] = new
    for rows in bands:
        low[rows, :] = x[rows, :].astype(BF16)
    for rows in bands:
        square[rows, :B] = dot(low[rows, :], low[:, :B]).astype(BF16)
    for i, rows in enumerate(bands):
        sign = 1.5 * raw[rows, :B] - 0.5 * dot(low[rows, :], square[:, :B])
        if i == 0:
            at = lax.broadcasted_iota(jnp.int32, (tall, B), 0) == lax.broadcasted_iota(jnp.int32, (tall, B), 1)
            sign = sign + jnp.where(at, 1.0, 0.0)
        out[rows, :] = 0.5 * sign


def sign_columns(codes, blocks):
    n = MAXB * B
    vmem = pl.BlockSpec(memory_space=pltpu.VMEM)
    half = pltpu.VMEM((n, n), BF16)
    full = pltpu.VMEM((n, n), F32)
    return pl.pallas_call(
        sign_kernel,
        out_shape=jax.ShapeDtypeStruct((n, B), F32),
        in_specs=[pl.BlockSpec(memory_space=pltpu.SMEM), vmem],
        out_specs=vmem,
        scratch_shapes=[full, half, half, full],
        compiler_params=pltpu.CompilerParams(vmem_limit_bytes=40 << 20),
        name="sign_columns",
    )(codes, blocks)


def solution(mesh):
    n_atoms, n_grid = mesh.shape["atoms"], mesh.shape["grid"]

    def shards(basis_values, potential, block_lists):
        blocks = exchange(basis_values[0, 0], potential[0], n_atoms, n_grid)
        return sign_columns(block_lists[0, 0], blocks)[None, None]

    placed = (P("atoms", "grid", None, None), P("atoms", "grid", None), P("atoms", "grid", None))
    return jax.shard_map(
        shards, mesh=mesh, in_specs=placed, out_specs=P("atoms", "grid", None, None), check_vma=False
    )
```

```python
import jax
import jax.numpy as jnp
from jax import lax
from jax.experimental import pallas as pl
from jax.experimental.pallas import tpu as pltpu
from jax.sharding import PartitionSpec as P

MAXB = 6
B = 128
MESH = pl.DeviceIdType.MESH
F32 = jnp.float32
BF16 = jnp.bfloat16

LEFT_ROWS, OWN_ROWS, RIGHT_ROWS, LEFT_PAIR, OWN_PAIR, WIDE_PAIR = 0, 6, 12, 18, 27, 36


def sym_index(i, j):
    return i * 3 + j - i * (i + 1) // 2


class PairType:
    def __init__(self, number, symmetric, base, distances):
        self.number, self.symmetric, self.base = number, symmetric, base
        self.size = 6 if symmetric else 9
        self.keys = [
            (i, j) for i in range(3) for j in range(3)
            if abs(i - j) in distances and (i <= j or not symmetric)
        ]
        self.down = [key for key in ((1, 1), (0, 1), (1, 0)) if key in self.keys]
        self.up = [key for key in ((1, 2), (2, 1)) if key in self.keys]

    def at(self, i, j):
        return sym_index(i, j) if self.symmetric else i * 3 + j


TYPES = [
    PairType(0, True, OWN_ROWS, (0, 1, 2)),
    PairType(1, False, OWN_PAIR, (0, 2)),
    PairType(2, False, WIDE_PAIR, (0, 1, 2)),
    PairType(3, False, LEFT_PAIR, (1,)),
]


def exchange_kernel(
    n_atoms, n_grid, values, potential, out,
    weighted, send_ll, send_rr, send_lc, send_cr, q0, q1, q2, q3,
    got_ll, got_rr, got_lc, got_cr, got_down, got_up, got_mid, got_far_down, got_far_up, mid, far, v,
    send_sem, recv_sem, load_sem,
):
    loads = []
    for n, group in enumerate((0, 2, 1)):
        cols = slice(group * 384, group * 384 + 384)
        loads.append(pltpu.make_async_copy(values.at[:, cols], v.at[:, cols], load_sem.at[n]))
        loads[-1].start()
    a = lax.axis_index("atoms")
    r = lax.axis_index("grid")
    last = n_grid - 1
    half = n_atoms // 2
    left, right = lax.rem(a + n_atoms - 1, n_atoms), lax.rem(a + 1, n_atoms)
    below, above = jnp.maximum(r - 1, 0), jnp.minimum(r + 1, last)
    below2, above2 = jnp.maximum(r - 2, 0), jnp.minimum(r + 2, last)
    has_below, has_above = r >= 1, r < last
    has_below2, has_above2 = r >= 2, r < last - 1
    odd = lax.rem(r, 2) == 1
    even = jnp.logical_not(odd)
    first_half, last_half = lax.rem(a, half) == 0, lax.rem(a, half) == half - 1
    at_wrap = jnp.logical_or(first_half, last_half)
    across = jnp.where(first_half, left, right)

    barrier = pltpu.get_barrier_semaphore()
    for peer in (left, right):
        pl.semaphore_signal(barrier, inc=1, device_id=(peer, r), device_id_type=MESH)
    peers = 2
    for exists, peer in (
        (has_below, (a, below)), (has_above, (a, above)), (has_below2, (a, below2)), (has_above2, (a, above2)),
        (jnp.logical_and(at_wrap, has_below), (across, below)), (jnp.logical_and(at_wrap, has_above), (across, above)),
    ):
        @pl.when(exists)
        def _():
            pl.semaphore_signal(barrier, inc=1, device_id=peer, device_id_type=MESH)
        peers = peers + jnp.where(exists, 1, 0)

    next_send, next_recv = [0], [0]
    sent = []

    def receives(n):
        next_recv[0] += n
        return next_recv[0] - n

    def when(condition, step):
        if condition is None:
            step()
        else:
            pl.when(condition)(step)

    def copy(src, dst, device, exists, recv):
        c = pltpu.make_async_remote_copy(
            src_ref=src, dst_ref=dst, send_sem=send_sem.at[next_send[0]], recv_sem=recv_sem.at[recv],
            device_id=device, device_id_type=MESH,
        )
        next_send[0] += 1
        when(exists, c.start)
        sent.append((c, exists))
        return sent[-1]

    def flush(copies):
        for entry in copies:
            c, exists = entry
            when(exists, c.wait_send)
            sent[:] = [other for other in sent if other is not entry]

    def arrival(dst, recv):
        return pltpu.make_async_remote_copy(
            src_ref=mid.at[0], dst_ref=dst, send_sem=send_sem.at[0], recv_sem=recv_sem.at[recv],
            device_id=(right, r), device_id_type=MESH,
        )

    def valid(key):
        low, high = min(key) > 0, max(key) < 2
        if low and high:
            return None
        if low:
            return has_above
        return has_below if high else jnp.logical_and(has_below, has_above)

    def choose(wrapped, ours, theirs):
        ours = True if ours is None else ours
        theirs = True if theirs is None else theirs
        return jnp.logical_or(jnp.logical_and(wrapped, theirs), jnp.logical_and(jnp.logical_not(wrapped), ours))

    def other(key):
        if max(key) == 2 and min(key) == 0:
            return key, r
        if max(key) == 2:
            return (key[0] - 1, key[1] - 1), above
        return (key[0] + 1, key[1] + 1), below

    class Reduce:
        def __init__(self, src, got, t, peer, wrapped, receives_wrapped):
            self.src, self.got, self.t, self.peer = src, got, t, peer
            self.wrapped, self.receives_wrapped = wrapped, receives_wrapped
            self.extra = t.size
            self.recv = receives(self.extra + 1)

        def send(self, key):
            t = self.t
            slot = t.at(*key)
            if key == (1, 1):
                theirs = jnp.where(even, t.at(0, 0), t.at(2, 2))
                cell = jnp.where(even, above, below)
            else:
                moved, cell = other(key)
                theirs = self.extra if key == (0, 0) else t.at(*moved)
            to = jnp.where(self.wrapped, theirs, slot)
            copy(
                self.src.at[slot], self.got.at[to],
                (self.peer, jnp.where(self.wrapped, cell, r)), valid(key), self.recv + to,
            )

        def add(self, key, q):
            t = self.t
            slot = t.at(*key)
            ours = valid(key)
            theirs = {(0, 0): odd, (2, 2): even, (1, 1): has_below}.get(key, ours)
            arrives = ours if theirs is ours else choose(self.receives_wrapped, ours, theirs)

            def step():
                arrival(self.got.at[slot], self.recv + slot).wait_recv()
                q[slot] = q[slot] + self.got[slot]

            when(arrives, step)
            if key == (1, 1):
                @pl.when(jnp.logical_and(self.receives_wrapped, has_above))
                def _():
                    arrival(self.got.at[self.extra], self.recv + self.extra).wait_recv()
                    q[slot] = q[slot] + self.got[self.extra]

    class Gather:
        def __init__(self, t, base, peer, wrapped):
            self.t, self.base, self.peer, self.wrapped = t, base, peer, wrapped
            self.recv = receives(t.size)

        def send(self, key):
            t = self.t
            src = out.at[t.base + t.at(*key)]

            def go(slot, cell, exists):
                copy(src, out.at[self.base + slot], (self.peer, cell), exists, self.recv + slot)

            slot = t.at(*key)
            if key == (1, 1):
                go(
                    jnp.where(self.wrapped, t.at(0, 0), slot), jnp.where(self.wrapped, above, r),
                    choose(self.wrapped, None, has_above),
                )
                go(t.at(2, 2), below, jnp.logical_and(self.wrapped, has_below))
                return
            moved, cell = other(key)
            ours = valid(key)
            theirs = {(0, 0): odd, (2, 2): even}.get(key, ours)
            go(
                jnp.where(self.wrapped, t.at(*moved), slot), jnp.where(self.wrapped, cell, r),
                ours if theirs is ours else choose(self.wrapped, ours, theirs),
            )

        def wait(self):
            for key in self.t.keys:
                slot = self.t.at(*key)
                when(valid(key), arrival(out.at[self.base + slot], self.recv + slot).wait_recv)

    def weigh(group):
        for part in range(4):
            rows = slice(part * 512, part * 512 + 512)
            turned = v[rows, group * 384:group * 384 + 384].T
            weighted[:, rows] = (turned.astype(F32) * potential[:, rows]).astype(BF16)

    def product(group, other, *places):
        block = jnp.dot(weighted[...], v[:, other * 384:other * 384 + 384], preferred_element_type=F32)
        for t, dst in places:
            for i, j in t.keys:
                dst[t.at(i, j)] = block[i * B:i * B + B, j * B:j * B + B]

    q = [q0, q1, q2, q3]

    class Line:
        def __init__(self, t, done):
            self.t, self.done = t, done
            self.recv = receives(8)

        def start(self, key):
            t, num, mine, recv = self.t, self.t.number, q[self.t.number], self.recv
            src = mine.at[t.at(*key)]
            started = []
            if key == (0, 0):
                copy(src, got_far_down.at[num], (a, below2), has_below2, recv)
                copy(src, got_mid.at[num], (a, below), r == 1, recv + 6)
            if key in t.down:
                n = t.down.index(key)
                started.append(copy(src, got_down.at[num * 3 + n], (a, below), has_below, recv + 1 + n))
            if key in t.up:
                n = t.up.index(key)
                started.append(copy(src, got_up.at[num * 2 + n], (a, above), has_above, recv + 4 + n))
            if key == (1, 1):
                copy(src, got_far_up.at[num], (a, above), r == 0, recv + 7)
            if key in ((0, 2), (2, 0)):
                self.put(key, src[...])
            return started

        def send_mid(self):
            t, num, mine, recv = self.t, self.t.number, q[self.t.number], self.recv
            when(has_above2, arrival(got_far_down.at[num], recv).wait_recv)
            mid[num] = mine[t.at(2, 2)] + got_far_down[num]
            return [copy(mid.at[num], got_mid.at[num], (a, above), has_above, recv + 6)]

        def send_far(self):
            t, num, mine, recv = self.t, self.t.number, q[self.t.number], self.recv
            when(has_above, arrival(got_down.at[num * 3], recv + 1).wait_recv)
            far[num] = mine[t.at(2, 2)] + got_down[num * 3]
            copy(far.at[num], got_far_up.at[num], (a, above2), has_above2, recv + 7)

        def put(self, key, value):
            out[self.t.base + self.t.at(*key)] = value
            self.done(key)

        def sides(self):
            t, num, mine, recv = self.t, self.t.number, q[self.t.number], self.recv
            for n, (i, j) in enumerate(t.down):
                if (i, j) == (1, 1):
                    continue
                when(has_above, arrival(got_down.at[num * 3 + n], recv + 1 + n).wait_recv)
                self.put((i + 1, j + 1), mine[t.at(i + 1, j + 1)] + got_down[num * 3 + n])
            for n, (i, j) in enumerate(t.up):
                when(has_below, arrival(got_up.at[num * 2 + n], recv + 4 + n).wait_recv)
                self.put((i - 1, j - 1), mine[t.at(i - 1, j - 1)] + got_up[num * 2 + n])

        def high(self):
            t, num = self.t, self.t.number
            self.put((2, 2), far[num] + got_far_down[num])

        def centre(self):
            t, num, mine, recv = self.t, self.t.number, q[self.t.number], self.recv
            arrival(got_mid.at[num], recv + 6).wait_recv()
            self.put((1, 1), mine[t.at(1, 1)] + got_mid[num])

        def low(self):
            t, num, mine, recv = self.t, self.t.number, q[self.t.number], self.recv
            when(has_below, arrival(got_far_up.at[num], recv + 7).wait_recv)
            self.put((0, 0), mine[t.at(0, 0)] + got_far_up[num])

    t0, t1, t2, t3 = TYPES
    pair_right = Gather(t1, LEFT_PAIR, right, last_half)
    pair_left = Gather(t3, OWN_PAIR, left, first_half)
    rows_right = Gather(t0, LEFT_ROWS, right, last_half)
    rows_left = Gather(t0, RIGHT_ROWS, left, first_half)

    def rows_done(key):
        rows_right.send(key)
        rows_left.send(key)

    line0, line1, line2 = Line(t0, rows_done), Line(t1, pair_right.send), Line(t2, lambda key: None)
    line3 = Line(t3, pair_left.send)
    lc = Reduce(send_lc, got_lc, t1, left, first_half, last_half)
    cr = Reduce(send_cr, got_cr, t3, right, last_half, first_half)
    ll = Reduce(send_ll, got_ll, t0, left, first_half, last_half)
    rr = Reduce(send_rr, got_rr, t0, right, last_half, first_half)

    @pl.when(jnp.logical_not(has_above2))
    def _():
        for num in range(3):
            got_far_down[num] = jnp.zeros((B, B), F32)

    def in_order(t):
        return [key for key in ((0, 0), (1, 1), (0, 1), (1, 0), (1, 2), (2, 1), (2, 2), (0, 2), (2, 0)) if key in t.keys]

    loads[0].wait()
    weigh(0)
    loads[1].wait()
    product(0, 2, (t2, q2))
    pl.semaphore_wait(barrier, peers)
    for key in in_order(t2):
        line2.start(key)
    product(0, 0, (t0, send_ll))
    for key in in_order(t0):
        ll.send(key)
    loads[2].wait()
    product(0, 1, (t1, send_lc), (t3, q3))
    for key in in_order(t1):
        lc.send(key)
    weigh(2)
    product(2, 2, (t0, send_rr))
    for key in in_order(t0):
        rr.send(key)
    weigh(1)
    product(1, 2, (t1, q1), (t3, send_cr))
    for key in in_order(t3):
        cr.send(key)
    product(1, 1, (t0, q0))
    line2.send_far()
    first = []
    for key in ((0, 0), (1, 1)):
        ll.add(key, q0)
        rr.add(key, q0)
        first += line0.start(key)
    for key in ((0, 0), (1, 1)):
        lc.add(key, q1)
        first += line1.start(key)
    for key in ((2, 2), (0, 1), (1, 2), (0, 2)):
        ll.add(key, q0)
        rr.add(key, q0)
    middle = line0.send_mid()
    for key in ((2, 2), (0, 2), (2, 0)):
        lc.add(key, q1)
    middle += line1.send_mid()
    line0.start((0, 2))
    line1.start((0, 2))
    line1.start((2, 0))
    for key in in_order(t3):
        cr.add(key, q3)
    flush(first)
    sides = []
    for key in ((0, 1), (1, 2)):
        sides += line0.start(key)
    for key in ((0, 1), (1, 0)):
        sides += line3.start(key)
    line0.send_far()
    line1.send_far()
    line0.high()
    line1.high()
    flush(middle)
    for key in ((1, 2), (2, 1)):
        line3.start(key)
    line2.send_mid()
    line0.centre()
    line1.centre()
    line0.low()
    line1.low()
    line0.sides()
    line3.sides()
    line2.sides()
    line2.high()
    line2.centre()
    line2.low()
    for gather in (pair_right, pair_left, rows_right, rows_left):
        gather.wait()
    for c, exists in sent:
        when(exists, c.wait_send)


COPIES = 128


def exchange(values, potential, n_atoms, n_grid):
    def blocks(n):
        return pltpu.VMEM((n, B, B), F32)

    vmem = pl.BlockSpec(memory_space=pltpu.VMEM)
    return pl.pallas_call(
        lambda *refs: exchange_kernel(n_atoms, n_grid, *refs),
        out_shape=jax.ShapeDtypeStruct((45, B, B), F32),
        in_specs=[pl.BlockSpec(memory_space=pl.ANY), vmem],
        out_specs=vmem,
        scratch_shapes=[
            pltpu.VMEM((3 * B, values.shape[0]), BF16),
            blocks(6), blocks(6), blocks(9), blocks(9), blocks(6), blocks(9), blocks(9), blocks(9),
            blocks(7), blocks(7), blocks(10), blocks(10), blocks(12), blocks(8), blocks(3), blocks(3), blocks(3), blocks(3), blocks(3),
            pltpu.VMEM(values.shape, BF16),
            pltpu.SemaphoreType.DMA((COPIES,)),
            pltpu.SemaphoreType.DMA((COPIES,)),
            pltpu.SemaphoreType.DMA((3,)),
        ],
        compiler_params=pltpu.CompilerParams(
            collective_id=0, has_side_effects=True, vmem_limit_bytes=48 << 20
        ),
        name="exchange",
    )(values, potential)


def sign_kernel(codes, blocks, out, raw, low, square, x):
    n = MAXB * B
    live = jnp.int32(0)
    for s in range(MAXB):
        live = live + jnp.where(codes[s] >= 0, 1, 0)

    def block_of(first, second):
        a1, i = first // 3, lax.rem(first, 3)
        a2, j = second // 3, lax.rem(second, 3)
        same = 6 * a1 + i * 3 + j - i * (i + 1) // 2
        apart = jnp.where(a2 - a1 == 2, WIDE_PAIR, LEFT_PAIR + 9 * a1) + i * 3 + j
        return jnp.where(a1 == a2, same, apart)

    eye = lax.broadcasted_iota(jnp.int32, (B, B), 0) == lax.broadcasted_iota(jnp.int32, (B, B), 1)
    zero = jnp.zeros((B, B), F32)
    diagonal = jnp.zeros((B, B), F32)
    for s in range(MAXB):
        cs = jnp.maximum(codes[s], 0)
        diagonal = diagonal + jnp.where(codes[s] >= 0, blocks[block_of(cs, cs)], zero)
    trace = jnp.sum(jnp.where(eye, diagonal, zero), keepdims=True)
    count = jnp.full((1, 1), live * B, jnp.int32).astype(F32)
    mean = trace / count
    once, twice = zero, zero
    for s in range(MAXB):
        for t in range(s, MAXB):
            cs, ct = jnp.maximum(codes[s], 0), jnp.maximum(codes[t], 0)
            used = codes[t] >= 0
            blk = jnp.where(used, blocks[block_of(jnp.minimum(cs, ct), jnp.maximum(cs, ct))], zero)
            rows, cols = slice(s * B, s * B + B), slice(t * B, t * B + B)
            if s == t:
                blk = blk - jnp.where(eye, jnp.where(used, mean, 0.0), zero)
                once = once + blk * blk
                raw[rows, cols] = blk
                low[rows, cols] = blk.astype(BF16)
            else:
                turned = blk.T
                twice = twice + blk * blk
                ordered = cs < ct
                here, there = jnp.where(ordered, blk, turned), jnp.where(ordered, turned, blk)
                raw[rows, cols] = here
                raw[cols, rows] = there
                low[rows, cols] = here.astype(BF16)
                low[cols, rows] = there.astype(BF16)
    total = jnp.sum(once + 2.0 * twice, keepdims=True)
    scale = -lax.rsqrt(total + 1e-06) * jnp.sqrt(count)
    tall = 256
    bands = [slice(i * tall, i * tall + tall) for i in range(n // tall)]

    def dot(p, q):
        return jnp.dot(p, q, preferred_element_type=F32)

    for rows in bands:
        square[rows, :] = (scale * scale * dot(low[rows, :], low[...])).astype(BF16)
    norm = jnp.zeros((1, 1), F32)
    for i, rows in enumerate(bands):
        f = dot(square[rows, :], square[:, i * tall:])
        norm = norm + jnp.sum(f[:, :tall] * f[:, :tall], keepdims=True)
        if i + 1 < len(bands):
            norm = norm + 2.0 * jnp.sum(f[:, tall:] * f[:, tall:], keepdims=True)
    rho = jnp.sqrt(jnp.sqrt(jnp.sqrt(norm + 1e-06)))
    inverse = 1.0 / rho
    linear, cubic = 1.5 * inverse * scale, 0.5 * inverse * inverse * inverse * scale
    for rows in bands:
        new = linear * raw[rows, :] - cubic * dot(low[rows, :], square[...])
        x[rows, :] = new
    for rows in bands:
        low[rows, :] = x[rows, :].astype(BF16)
    for rows in bands:
        square[rows, :] = dot(low[rows, :], low[...]).astype(BF16)
    for rows in bands:
        new = 1.5 * x[rows, :] - 0.5 * dot(low[rows, :], square[...])
        raw[rows, :B] = new[:, :B]
        x[rows, :] = new
    for rows in bands:
        low[rows, :] = x[rows, :].astype(BF16)
    for rows in bands:
        square[rows, :B] = dot(low[rows, :], low[:, :B]).astype(BF16)
    for i, rows in enumerate(bands):
        sign = 1.5 * raw[rows, :B] - 0.5 * dot(low[rows, :], square[:, :B])
        if i == 0:
            at = lax.broadcasted_iota(jnp.int32, (tall, B), 0) == lax.broadcasted_iota(jnp.int32, (tall, B), 1)
            sign = sign + jnp.where(at, 1.0, 0.0)
        out[rows, :] = 0.5 * sign


def sign_columns(codes, blocks):
    n = MAXB * B
    vmem = pl.BlockSpec(memory_space=pltpu.VMEM)
    half = pltpu.VMEM((n, n), BF16)
    full = pltpu.VMEM((n, n), F32)
    return pl.pallas_call(
        sign_kernel,
        out_shape=jax.ShapeDtypeStruct((n, B), F32),
        in_specs=[pl.BlockSpec(memory_space=pltpu.SMEM), vmem],
        out_specs=vmem,
        scratch_shapes=[full, half, half, full],
        compiler_params=pltpu.CompilerParams(vmem_limit_bytes=40 << 20),
        name="sign_columns",
    )(codes, blocks)


def solution(mesh):
    n_atoms, n_grid = mesh.shape["atoms"], mesh.shape["grid"]

    def shards(basis_values, potential, block_lists):
        blocks = exchange(basis_values[0, 0], potential[0], n_atoms, n_grid)
        return sign_columns(block_lists[0, 0], blocks)[None, None]

    placed = (P("atoms", "grid", None, None), P("atoms", "grid", None), P("atoms", "grid", None))
    return jax.shard_map(
        shards, mesh=mesh, in_specs=placed, out_specs=P("atoms", "grid", None, None), check_vma=False
    )
```

```python
import jax
import jax.numpy as jnp
from jax import lax
from jax.experimental import pallas as pl
from jax.experimental.pallas import tpu as pltpu
from jax.sharding import PartitionSpec as P

MAXB = 6
B = 128
MESH = pl.DeviceIdType.MESH
F32 = jnp.float32
BF16 = jnp.bfloat16

LEFT_ROWS, OWN_ROWS, RIGHT_ROWS, LEFT_PAIR, OWN_PAIR, WIDE_PAIR = 0, 6, 12, 18, 27, 36


def sym_index(i, j):
    return i * 3 + j - i * (i + 1) // 2


class PairType:
    def __init__(self, number, symmetric, base, distances):
        self.number, self.symmetric, self.base = number, symmetric, base
        self.size = 6 if symmetric else 9
        self.keys = [
            (i, j) for i in range(3) for j in range(3)
            if abs(i - j) in distances and (i <= j or not symmetric)
        ]
        self.down = [key for key in ((1, 1), (0, 1), (1, 0)) if key in self.keys]
        self.up = [key for key in ((1, 2), (2, 1)) if key in self.keys]

    def at(self, i, j):
        return sym_index(i, j) if self.symmetric else i * 3 + j


TYPES = [
    PairType(0, True, OWN_ROWS, (0, 1, 2)),
    PairType(1, False, OWN_PAIR, (0, 2)),
    PairType(2, False, WIDE_PAIR, (0, 1, 2)),
    PairType(3, False, LEFT_PAIR, (1,)),
]


def exchange_kernel(
    n_atoms, n_grid, values, potential, out,
    weighted, send_ll, send_rr, send_lc, send_cr, q0, q1, q2, q3,
    got_ll, got_rr, got_lc, got_cr, got_down, got_up, got_mid, got_far_down, got_far_up, mid, far, v,
    send_sem, recv_sem, load_sem,
):
    loads = []
    for n, group in enumerate((0, 2, 1)):
        cols = slice(group * 384, group * 384 + 384)
        loads.append(pltpu.make_async_copy(values.at[:, cols], v.at[:, cols], load_sem.at[n]))
        loads[-1].start()
    a = lax.axis_index("atoms")
    r = lax.axis_index("grid")
    last = n_grid - 1
    half = n_atoms // 2
    left, right = lax.rem(a + n_atoms - 1, n_atoms), lax.rem(a + 1, n_atoms)
    below, above = jnp.maximum(r - 1, 0), jnp.minimum(r + 1, last)
    below2, above2 = jnp.maximum(r - 2, 0), jnp.minimum(r + 2, last)
    has_below, has_above = r >= 1, r < last
    has_below2, has_above2 = r >= 2, r < last - 1
    odd = lax.rem(r, 2) == 1
    even = jnp.logical_not(odd)
    first_half, last_half = lax.rem(a, half) == 0, lax.rem(a, half) == half - 1
    at_wrap = jnp.logical_or(first_half, last_half)
    across = jnp.where(first_half, left, right)

    barrier = pltpu.get_barrier_semaphore()
    for peer in (left, right):
        pl.semaphore_signal(barrier, inc=1, device_id=(peer, r), device_id_type=MESH)
    peers = 2
    for exists, peer in (
        (has_below, (a, below)), (has_above, (a, above)), (has_below2, (a, below2)), (has_above2, (a, above2)),
        (jnp.logical_and(at_wrap, has_below), (across, below)), (jnp.logical_and(at_wrap, has_above), (across, above)),
    ):
        @pl.when(exists)
        def _():
            pl.semaphore_signal(barrier, inc=1, device_id=peer, device_id_type=MESH)
        peers = peers + jnp.where(exists, 1, 0)

    next_send, next_recv = [0], [0]
    sent = []

    def receives(n):
        next_recv[0] += n
        return next_recv[0] - n

    def when(condition, step):
        if condition is None:
            step()
        else:
            pl.when(condition)(step)

    def copy(src, dst, device, exists, recv):
        c = pltpu.make_async_remote_copy(
            src_ref=src, dst_ref=dst, send_sem=send_sem.at[next_send[0]], recv_sem=recv_sem.at[recv],
            device_id=device, device_id_type=MESH,
        )
        next_send[0] += 1
        when(exists, c.start)
        sent.append((c, exists))
        return sent[-1]

    def flush(copies):
        for entry in copies:
            c, exists = entry
            when(exists, c.wait_send)
            sent[:] = [other for other in sent if other is not entry]

    def arrival(dst, recv):
        return pltpu.make_async_remote_copy(
            src_ref=mid.at[0], dst_ref=dst, send_sem=send_sem.at[0], recv_sem=recv_sem.at[recv],
            device_id=(right, r), device_id_type=MESH,
        )

    def valid(key):
        low, high = min(key) > 0, max(key) < 2
        if low and high:
            return None
        if low:
            return has_above
        return has_below if high else jnp.logical_and(has_below, has_above)

    def choose(wrapped, ours, theirs):
        ours = True if ours is None else ours
        theirs = True if theirs is None else theirs
        return jnp.logical_or(jnp.logical_and(wrapped, theirs), jnp.logical_and(jnp.logical_not(wrapped), ours))

    def other(key):
        if max(key) == 2 and min(key) == 0:
            return key, r
        if max(key) == 2:
            return (key[0] - 1, key[1] - 1), above
        return (key[0] + 1, key[1] + 1), below

    class Reduce:
        def __init__(self, src, got, t, peer, wrapped, receives_wrapped):
            self.src, self.got, self.t, self.peer = src, got, t, peer
            self.wrapped, self.receives_wrapped = wrapped, receives_wrapped
            self.extra = t.size
            self.recv = receives(self.extra + 1)

        def send(self, key):
            t = self.t
            slot = t.at(*key)
            if key == (1, 1):
                theirs = jnp.where(even, t.at(0, 0), t.at(2, 2))
                cell = jnp.where(even, above, below)
            else:
                moved, cell = other(key)
                theirs = self.extra if key == (0, 0) else t.at(*moved)
            to = jnp.where(self.wrapped, theirs, slot)
            copy(
                self.src.at[slot], self.got.at[to],
                (self.peer, jnp.where(self.wrapped, cell, r)), valid(key), self.recv + to,
            )

        def add(self, key, q):
            t = self.t
            slot = t.at(*key)
            ours = valid(key)
            theirs = {(0, 0): odd, (2, 2): even, (1, 1): has_below}.get(key, ours)
            arrives = ours if theirs is ours else choose(self.receives_wrapped, ours, theirs)

            def step():
                arrival(self.got.at[slot], self.recv + slot).wait_recv()
                q[slot] = q[slot] + self.got[slot]

            when(arrives, step)
            if key == (1, 1):
                @pl.when(jnp.logical_and(self.receives_wrapped, has_above))
                def _():
                    arrival(self.got.at[self.extra], self.recv + self.extra).wait_recv()
                    q[slot] = q[slot] + self.got[self.extra]

    class Gather:
        def __init__(self, t, base, peer, wrapped):
            self.t, self.base, self.peer, self.wrapped = t, base, peer, wrapped
            self.recv = receives(t.size)

        def send(self, key):
            t = self.t
            src = out.at[t.base + t.at(*key)]

            def go(slot, cell, exists):
                copy(src, out.at[self.base + slot], (self.peer, cell), exists, self.recv + slot)

            slot = t.at(*key)
            if key == (1, 1):
                go(
                    jnp.where(self.wrapped, t.at(0, 0), slot), jnp.where(self.wrapped, above, r),
                    choose(self.wrapped, None, has_above),
                )
                go(t.at(2, 2), below, jnp.logical_and(self.wrapped, has_below))
                return
            moved, cell = other(key)
            ours = valid(key)
            theirs = {(0, 0): odd, (2, 2): even}.get(key, ours)
            go(
                jnp.where(self.wrapped, t.at(*moved), slot), jnp.where(self.wrapped, cell, r),
                ours if theirs is ours else choose(self.wrapped, ours, theirs),
            )

        def wait(self):
            for key in self.t.keys:
                slot = self.t.at(*key)
                when(valid(key), arrival(out.at[self.base + slot], self.recv + slot).wait_recv)

    def weigh(group):
        for part in range(4):
            rows = slice(part * 512, part * 512 + 512)
            turned = v[rows, group * 384:group * 384 + 384].T
            weighted[:, rows] = (turned.astype(F32) * potential[:, rows]).astype(BF16)

    def product(group, other, *places):
        block = jnp.dot(weighted[...], v[:, other * 384:other * 384 + 384], preferred_element_type=F32)
        for t, dst in places:
            for i, j in t.keys:
                dst[t.at(i, j)] = block[i * B:i * B + B, j * B:j * B + B]

    q = [q0, q1, q2, q3]

    class Line:
        def __init__(self, t, done):
            self.t, self.done = t, done
            self.recv = receives(8)

        def start(self, key):
            t, num, mine, recv = self.t, self.t.number, q[self.t.number], self.recv
            src = mine.at[t.at(*key)]
            started = []
            if key == (0, 0):
                copy(src, got_far_down.at[num], (a, below2), has_below2, recv)
                copy(src, got_mid.at[num], (a, below), r == 1, recv + 6)
            if key in t.down:
                n = t.down.index(key)
                started.append(copy(src, got_down.at[num * 3 + n], (a, below), has_below, recv + 1 + n))
            if key in t.up:
                n = t.up.index(key)
                started.append(copy(src, got_up.at[num * 2 + n], (a, above), has_above, recv + 4 + n))
            if key == (1, 1):
                copy(src, got_far_up.at[num], (a, above), r == 0, recv + 7)
            if key in ((0, 2), (2, 0)):
                self.put(key, src[...])
            return started

        def send_mid(self):
            t, num, mine, recv = self.t, self.t.number, q[self.t.number], self.recv
            when(has_above2, arrival(got_far_down.at[num], recv).wait_recv)
            mid[num] = mine[t.at(2, 2)] + got_far_down[num]
            return [copy(mid.at[num], got_mid.at[num], (a, above), has_above, recv + 6)]

        def send_far(self):
            t, num, mine, recv = self.t, self.t.number, q[self.t.number], self.recv
            when(has_above, arrival(got_down.at[num * 3], recv + 1).wait_recv)
            far[num] = mine[t.at(2, 2)] + got_down[num * 3]
            copy(far.at[num], got_far_up.at[num], (a, above2), has_above2, recv + 7)

        def put(self, key, value):
            out[self.t.base + self.t.at(*key)] = value
            self.done(key)

        def sides(self):
            t, num, mine, recv = self.t, self.t.number, q[self.t.number], self.recv
            for n, (i, j) in enumerate(t.down):
                if (i, j) == (1, 1):
                    continue
                when(has_above, arrival(got_down.at[num * 3 + n], recv + 1 + n).wait_recv)
                self.put((i + 1, j + 1), mine[t.at(i + 1, j + 1)] + got_down[num * 3 + n])
            for n, (i, j) in enumerate(t.up):
                when(has_below, arrival(got_up.at[num * 2 + n], recv + 4 + n).wait_recv)
                self.put((i - 1, j - 1), mine[t.at(i - 1, j - 1)] + got_up[num * 2 + n])

        def high(self):
            t, num = self.t, self.t.number
            self.put((2, 2), far[num] + got_far_down[num])

        def centre(self):
            t, num, mine, recv = self.t, self.t.number, q[self.t.number], self.recv
            arrival(got_mid.at[num], recv + 6).wait_recv()
            self.put((1, 1), mine[t.at(1, 1)] + got_mid[num])

        def low(self):
            t, num, mine, recv = self.t, self.t.number, q[self.t.number], self.recv
            when(has_below, arrival(got_far_up.at[num], recv + 7).wait_recv)
            self.put((0, 0), mine[t.at(0, 0)] + got_far_up[num])

    t0, t1, t2, t3 = TYPES
    pair_right = Gather(t1, LEFT_PAIR, right, last_half)
    pair_left = Gather(t3, OWN_PAIR, left, first_half)
    rows_right = Gather(t0, LEFT_ROWS, right, last_half)
    rows_left = Gather(t0, RIGHT_ROWS, left, first_half)

    def rows_done(key):
        rows_right.send(key)
        rows_left.send(key)

    line0, line1, line2 = Line(t0, rows_done), Line(t1, pair_right.send), Line(t2, lambda key: None)
    line3 = Line(t3, pair_left.send)
    lc = Reduce(send_lc, got_lc, t1, left, first_half, last_half)
    cr = Reduce(send_cr, got_cr, t3, right, last_half, first_half)
    ll = Reduce(send_ll, got_ll, t0, left, first_half, last_half)
    rr = Reduce(send_rr, got_rr, t0, right, last_half, first_half)

    @pl.when(jnp.logical_not(has_above2))
    def _():
        for num in range(3):
            got_far_down[num] = jnp.zeros((B, B), F32)

    def in_order(t):
        return [key for key in ((0, 0), (1, 1), (0, 1), (1, 0), (1, 2), (2, 1), (2, 2), (0, 2), (2, 0)) if key in t.keys]

    loads[0].wait()
    weigh(0)
    loads[1].wait()
    product(0, 2, (t2, q2))
    pl.semaphore_wait(barrier, peers)
    for key in in_order(t2):
        line2.start(key)
    loads[2].wait()
    product(0, 1, (t1, send_lc), (t3, q3))
    for key in in_order(t1):
        lc.send(key)
    product(0, 0, (t0, send_ll))
    for key in in_order(t0):
        ll.send(key)
    weigh(2)
    product(2, 2, (t0, send_rr))
    for key in in_order(t0):
        rr.send(key)
    weigh(1)
    product(1, 2, (t1, q1), (t3, send_cr))
    for key in in_order(t3):
        cr.send(key)
    product(1, 1, (t0, q0))
    line2.send_far()
    first = []
    for key in ((0, 0), (1, 1)):
        ll.add(key, q0)
        rr.add(key, q0)
        first += line0.start(key)
    for key in ((0, 0), (1, 1)):
        lc.add(key, q1)
        first += line1.start(key)
    for key in ((2, 2), (0, 1), (1, 2), (0, 2)):
        ll.add(key, q0)
        rr.add(key, q0)
    middle = line0.send_mid()
    for key in ((2, 2), (0, 2), (2, 0)):
        lc.add(key, q1)
    middle += line1.send_mid()
    line0.start((0, 2))
    line1.start((0, 2))
    line1.start((2, 0))
    for key in in_order(t3):
        cr.add(key, q3)
    flush(first)
    sides = []
    for key in ((0, 1), (1, 2)):
        sides += line0.start(key)
    for key in ((0, 1), (1, 0)):
        sides += line3.start(key)
    line0.send_far()
    line1.send_far()
    line0.high()
    line1.high()
    flush(middle)
    for key in ((1, 2), (2, 1)):
        line3.start(key)
    line2.send_mid()
    line0.centre()
    line1.centre()
    line0.low()
    line1.low()
    line0.sides()
    line3.sides()
    line2.sides()
    line2.high()
    line2.centre()
    line2.low()
    for gather in (pair_right, pair_left, rows_right, rows_left):
        gather.wait()
    for c, exists in sent:
        when(exists, c.wait_send)


COPIES = 128


def exchange(values, potential, n_atoms, n_grid):
    def blocks(n):
        return pltpu.VMEM((n, B, B), F32)

    vmem = pl.BlockSpec(memory_space=pltpu.VMEM)
    return pl.pallas_call(
        lambda *refs: exchange_kernel(n_atoms, n_grid, *refs),
        out_shape=jax.ShapeDtypeStruct((45, B, B), F32),
        in_specs=[pl.BlockSpec(memory_space=pl.ANY), vmem],
        out_specs=vmem,
        scratch_shapes=[
            pltpu.VMEM((3 * B, values.shape[0]), BF16),
            blocks(6), blocks(6), blocks(9), blocks(9), blocks(6), blocks(9), blocks(9), blocks(9),
            blocks(7), blocks(7), blocks(10), blocks(10), blocks(12), blocks(8), blocks(3), blocks(3), blocks(3), blocks(3), blocks(3),
            pltpu.VMEM(values.shape, BF16),
            pltpu.SemaphoreType.DMA((COPIES,)),
            pltpu.SemaphoreType.DMA((COPIES,)),
            pltpu.SemaphoreType.DMA((3,)),
        ],
        compiler_params=pltpu.CompilerParams(
            collective_id=0, has_side_effects=True, vmem_limit_bytes=48 << 20
        ),
        name="exchange",
    )(values, potential)


def sign_kernel(codes, blocks, out, raw, low, square, x):
    n = MAXB * B
    live = jnp.int32(0)
    for s in range(MAXB):
        live = live + jnp.where(codes[s] >= 0, 1, 0)

    def block_of(first, second):
        a1, i = first // 3, lax.rem(first, 3)
        a2, j = second // 3, lax.rem(second, 3)
        same = 6 * a1 + i * 3 + j - i * (i + 1) // 2
        apart = jnp.where(a2 - a1 == 2, WIDE_PAIR, LEFT_PAIR + 9 * a1) + i * 3 + j
        return jnp.where(a1 == a2, same, apart)

    eye = lax.broadcasted_iota(jnp.int32, (B, B), 0) == lax.broadcasted_iota(jnp.int32, (B, B), 1)
    zero = jnp.zeros((B, B), F32)
    diagonal = jnp.zeros((B, B), F32)
    for s in range(MAXB):
        cs = jnp.maximum(codes[s], 0)
        diagonal = diagonal + jnp.where(codes[s] >= 0, blocks[block_of(cs, cs)], zero)
    trace = jnp.sum(jnp.where(eye, diagonal, zero), keepdims=True)
    count = jnp.full((1, 1), live * B, jnp.int32).astype(F32)
    mean = trace / count
    once, twice = zero, zero
    for s in range(MAXB):
        for t in range(s, MAXB):
            cs, ct = jnp.maximum(codes[s], 0), jnp.maximum(codes[t], 0)
            used = codes[t] >= 0
            blk = jnp.where(used, blocks[block_of(jnp.minimum(cs, ct), jnp.maximum(cs, ct))], zero)
            rows, cols = slice(s * B, s * B + B), slice(t * B, t * B + B)
            if s == t:
                blk = blk - jnp.where(eye, jnp.where(used, mean, 0.0), zero)
                once = once + blk * blk
                raw[rows, cols] = blk
                low[rows, cols] = blk.astype(BF16)
            else:
                turned = blk.T
                twice = twice + blk * blk
                ordered = cs < ct
                here, there = jnp.where(ordered, blk, turned), jnp.where(ordered, turned, blk)
                raw[rows, cols] = here
                raw[cols, rows] = there
                low[rows, cols] = here.astype(BF16)
                low[cols, rows] = there.astype(BF16)
    total = jnp.sum(once + 2.0 * twice, keepdims=True)
    scale = -lax.rsqrt(total + 1e-06) * jnp.sqrt(count)
    tall = 256
    bands = [slice(i * tall, i * tall + tall) for i in range(n // tall)]

    def dot(p, q):
        return jnp.dot(p, q, preferred_element_type=F32)

    for rows in bands:
        square[rows, :] = (scale * scale * dot(low[rows, :], low[...])).astype(BF16)
    norm = jnp.zeros((1, 1), F32)
    for i, rows in enumerate(bands):
        f = dot(square[rows, :], square[:, i * tall:])
        norm = norm + jnp.sum(f[:, :tall] * f[:, :tall], keepdims=True)
        if i + 1 < len(bands):
            norm = norm + 2.0 * jnp.sum(f[:, tall:] * f[:, tall:], keepdims=True)
    rho = jnp.sqrt(jnp.sqrt(jnp.sqrt(norm + 1e-06)))
    inverse = 1.0 / rho
    linear, cubic = 1.5 * inverse * scale, 0.5 * inverse * inverse * inverse * scale
    for rows in bands:
        new = linear * raw[rows, :] - cubic * dot(low[rows, :], square[...])
        x[rows, :] = new
    for rows in bands:
        low[rows, :] = x[rows, :].astype(BF16)
    for rows in bands:
        square[rows, :] = dot(low[rows, :], low[...]).astype(BF16)
    for rows in bands:
        new = 1.5 * x[rows, :] - 0.5 * dot(low[rows, :], square[...])
        raw[rows, :B] = new[:, :B]
        x[rows, :] = new
    for rows in bands:
        low[rows, :] = x[rows, :].astype(BF16)
    for rows in bands:
        square[rows, :B] = dot(low[rows, :], low[:, :B]).astype(BF16)
    for i, rows in enumerate(bands):
        sign = 1.5 * raw[rows, :B] - 0.5 * dot(low[rows, :], square[:, :B])
        if i == 0:
            at = lax.broadcasted_iota(jnp.int32, (tall, B), 0) == lax.broadcasted_iota(jnp.int32, (tall, B), 1)
            sign = sign + jnp.where(at, 1.0, 0.0)
        out[rows, :] = 0.5 * sign


def sign_columns(codes, blocks):
    n = MAXB * B
    vmem = pl.BlockSpec(memory_space=pltpu.VMEM)
    half = pltpu.VMEM((n, n), BF16)
    full = pltpu.VMEM((n, n), F32)
    return pl.pallas_call(
        sign_kernel,
        out_shape=jax.ShapeDtypeStruct((n, B), F32),
        in_specs=[pl.BlockSpec(memory_space=pltpu.SMEM), vmem],
        out_specs=vmem,
        scratch_shapes=[full, half, half, full],
        compiler_params=pltpu.CompilerParams(vmem_limit_bytes=40 << 20),
        name="sign_columns",
    )(codes, blocks)


def solution(mesh):
    n_atoms, n_grid = mesh.shape["atoms"], mesh.shape["grid"]

    def shards(basis_values, potential, block_lists):
        blocks = exchange(basis_values[0, 0], potential[0], n_atoms, n_grid)
        return sign_columns(block_lists[0, 0], blocks)[None, None]

    placed = (P("atoms", "grid", None, None), P("atoms", "grid", None), P("atoms", "grid", None))
    return jax.shard_map(
        shards, mesh=mesh, in_specs=placed, out_specs=P("atoms", "grid", None, None), check_vma=False
    )
```
